32 devices in a mesh: airway: 4 (over y, core), section: 8 (over z, x).
Axes of the slice: x: 2, y: 2, z: 4, core: 2. Of those that a mesh axis runs over, the one named last changes fastest.
Arguments:
- fluid_velocity: float32 [3, 64, 64, 1024], P(None, None, 'section', 'airway'), may hold values from -6 to 6
- viscosity: float32 [64, 1024], P('section', 'airway'), may hold values from 0.002 to 0.008
- axial_speed: float32 [64, 1024], P('section', 'airway'), may hold values from 0.01 to 0.04
- fluid_mass: float32 [64, 1024], P('section', 'airway'), may hold values from 2 to 8
- positions: float32 [3072, 3, 128], P(('airway', 'section')), may hold values from -1 to 1
- velocities: float32 [3072, 3, 128], P(('airway', 'section')), may hold values from -6 to 6
- relax_rates: float32 [3072, 128], P(('airway', 'section')), may hold values from 0.02 to 0.5
- bin_element: int32 [3072], P(('airway', 'section')), may hold values from 0 to 2047
- bin_fill: int32 [3072], P(('airway', 'section')), may hold values from 0 to 128, as said below
Outputs:
- fluid_out: float32 [3, 64, 64, 1024], P(None, None, 'section', 'airway')
- particles_out: float32 [3072, 6, 128], P(('airway', 'section'))
The draws below stay inside these ranges and needn't reach their ends.
Inputs may be any that keep to these rules, and one draw needn't show every extreme that they name: `bin_fill`: on each device the bins with particles are the first 64 + k slots, k from 0 to 32; over all devices the k sum to exactly 512, and k = 32 on some device. Every device's first slot holds 128 particles.
All inputs are finite; a program needn't handle non-finite values.
Results may differ from the reference program's by a relative error of at most 0.00023.
Values sent between devices are 32-bit elements; how exact they have to be, the bound alone decides.
No kernel may reach another device: no remote copies, remote signals or barrier semaphores. Data moves between devices by JAX's collectives and lax.ppermute only.
A program may use at most 64 MiB of HBM per device.

```python
import math
import jax
import jax.numpy as jnp
import numpy as np
from jax import lax

NODES = 64
PER_BIN = 128
SUBSTEPS = 16
PASSES = 4
EA_DEV = 256
ES_DEV = 8
HOME = 64
EA = 1024
ES = 64
OVER = 32
BINS_CAP = 96
NB = 3072
N_SECTION = 8


def draw_bin_fill(key, part):
    key_order = jax.random.fold_in(key, 101)
    key_shares = jax.random.fold_in(key, 202)
    key_counts = jax.random.fold_in(key, 303)
    device_order = jax.random.permutation(key_order, OVER)
    shares = jax.random.randint(key_shares, (OVER // 2,), 0, OVER + 1)
    shares = shares.at[0].set(OVER)
    overflow = jnp.zeros((OVER,), jnp.int32)
    overflow = overflow.at[device_order[0::2]].set(shares)
    overflow = overflow.at[device_order[1::2]].set(OVER - shares)
    occupied_slots = HOME + overflow
    slot_index = jnp.arange(BINS_CAP, dtype=jnp.int32)
    fill_counts = jax.random.randint(key_counts, (OVER, BINS_CAP), 1, PER_BIN + 1)
    fill_counts = fill_counts.at[:, 0].set(PER_BIN)
    result = jnp.where(slot_index[None, :] < occupied_slots[:, None], fill_counts, 0)
    return result.reshape(-1).astype(jnp.int32)


def set_ends(values, rng, smallest, high):
    spot = [jax.random.randint(jax.random.fold_in(rng, axis), (), 0, length) for axis, length in enumerate(values.shape)]
    main_axis = values.shape.index(max(values.shape))
    neighbour = spot[:main_axis] + [(spot[main_axis] + 1) % values.shape[main_axis]] + spot[main_axis + 1:]
    return values.at[tuple(spot)].set(smallest).at[tuple(neighbour)].set(high)


def block_scale(key, shape, cuts, smallest, largest):
    def one(dim, shards_of):
        steps = jax.random.uniform(jax.random.fold_in(jax.random.fold_in(key, 6), dim), (shards_of,), jnp.float32, smallest / len(cuts), largest / len(cuts))
        return jnp.repeat(jnp.exp(steps), shape[dim] // shards_of).reshape((-1,) + (1,) * (len(shape) - dim - 1))

    factor_of = one(*cuts[0])
    for cut in cuts[1:]:
        factor_of = factor_of * one(*cut)
    return factor_of


def noise(own_key, extent, deviation, bound, shards=(), kind=jnp.bfloat16):
    values = jax.random.normal(own_key, extent, jnp.float32) * deviation
    if len(shards) > 0:
        values = block_scale(own_key, extent, shards, -0.22, 0.18) * values
    return jnp.clip(values, min=-bound, max=bound).astype(kind)


def setup_inputs(seed: int = 0) -> dict:
    arg_keys = jax.random.split(jax.random.key(seed), 10)
    fluid_velocity = noise(arg_keys[0], (3, NODES, ES, EA), 1.0, 6.0, ((2, 8), (3, 4)), jnp.float32)
    viscosity = jnp.clip(jnp.exp(math.log(0.008) - 1.3862944 * jax.random.uniform(arg_keys[1], (ES, EA), jnp.float32) ** block_scale(arg_keys[1], (ES, EA), ((0, 8), (1, 4)), -0.2, 0.2)), 0.002, 0.008)
    axial_speed = jnp.clip(0.01 + 0.03 * jax.random.uniform(arg_keys[2], (ES, EA), jnp.float32) ** block_scale(arg_keys[2], (ES, EA), ((0, 8), (1, 4)), -0.2, 0.2), 0.01, 0.04)
    fluid_mass = jnp.clip(jnp.exp(math.log(8.0) - 1.3862944 * jax.random.uniform(arg_keys[3], (ES, EA), jnp.float32) ** block_scale(arg_keys[3], (ES, EA), ((0, 8), (1, 4)), -0.2, 0.2)), 2.0, 8.0)
    positions = jnp.clip(jax.random.uniform(arg_keys[4], (NB, 3, PER_BIN), jnp.float32, -1.0, 1.0) * block_scale(arg_keys[4], (NB, 3, PER_BIN), ((0, 32),), -0.4, 0.0), -1.0, 1.0)
    velocities = noise(arg_keys[5], (NB, 3, PER_BIN), 1.0, 6.0, ((0, 32),), jnp.float32)
    relax_rates = jnp.clip(jnp.exp(math.log(0.5) - 3.218876 * jax.random.uniform(arg_keys[6], (NB, PER_BIN), jnp.float32) ** block_scale(arg_keys[6], (NB, PER_BIN), ((0, 32),), -0.2, 0.2)), 0.02, 0.5)
    bin_element = set_ends(jax.random.randint(arg_keys[7], (NB,), 0, ES_DEV * EA_DEV), jax.random.fold_in(arg_keys[7], 1), 0, (ES_DEV * EA_DEV) - 1).astype(jnp.int32)
    bin_fill = draw_bin_fill(jax.random.fold_in(arg_keys[9], 71), 0)
    return {"fluid_velocity": fluid_velocity, "viscosity": viscosity, "axial_speed": axial_speed, "fluid_mass": fluid_mass, "positions": positions, "velocities": velocities, "relax_rates": relax_rates, "bin_element": bin_element, "bin_fill": bin_fill}


node_coords = (-1.0, -1.0 / 3.0, 1.0 / 3.0, 1.0)
penalty_weight = 0.25
stride_step = 0.05
exact_mode = lax.Precision.HIGHEST


def deriv_table():
    matrix = np.zeros((4, 4))
    for row_node in range(4):
        for col_node in range(4):
            summed = 0.0
            for skip_node in range(4):
                if skip_node != col_node:
                    factor = 1.0 / (node_coords[col_node] - node_coords[skip_node])
                    for third_node in range(4):
                        if third_node != col_node and third_node != skip_node:
                            factor = factor * (node_coords[row_node] - node_coords[third_node]) / (node_coords[col_node] - node_coords[third_node])
                    summed = summed + factor
            matrix[row_node, col_node] = summed
    return matrix


def operator_table():
    first_deriv = deriv_table()
    second_deriv = first_deriv @ first_deriv
    identity = np.eye(4)
    laplace = np.kron(np.kron(second_deriv, identity), identity) + np.kron(np.kron(identity, second_deriv), identity) + np.kron(np.kron(identity, identity), second_deriv)
    airway_grad = np.kron(np.kron(first_deriv, identity), identity)
    return np.concatenate([laplace, airway_grad], axis=0).astype(np.float32)


def basis_values(coordinate):
    values = []
    for centre in range(4):
        factor = jnp.ones_like(coordinate)
        for second in range(4):
            if second != centre:
                factor = factor * (coordinate - node_coords[second]) / (node_coords[centre] - node_coords[second])
        values.append(factor)
    return jnp.stack(values, axis=1)


def drag_bins(records, nodal_velocity):
    batch_size = records.shape[0]
    fluid_nodes = nodal_velocity.reshape(batch_size, 3, NODES)
    relax_rate = records[:, 6]
    occupied = records[:, 7]

    def substep(turn_index, carried):
        position, velocity, drag_sum, weight_sum = carried
        basis_one = basis_values(position[:, 0])
        basis_two = basis_values(position[:, 1])
        basis_three = basis_values(position[:, 2])
        weights = (basis_one[:, :, None, None, :] * basis_two[:, None, :, None, :] * basis_three[:, None, None, :, :]).reshape(batch_size, NODES, -1)
        at_particle = jnp.einsum("bcn,bnp->bcp", fluid_nodes, weights, precision=exact_mode)
        change = (relax_rate * occupied)[:, None, :] * (at_particle - velocity)
        velocity = velocity + change
        position = jnp.clip(position + stride_step * occupied[:, None, :] * velocity, -1.0, 1.0)
        drag_sum = drag_sum + jnp.einsum("bnp,bcp->bcn", weights, change, precision=exact_mode)
        weight_sum = weight_sum + jnp.einsum("bnp,bp->bn", weights * weights, occupied, precision=exact_mode)
        return position, velocity, drag_sum, weight_sum

    start_state = (records[:, 0:3], records[:, 3:6], jnp.zeros((batch_size, 3, NODES), jnp.float32), jnp.zeros((batch_size, NODES), jnp.float32))
    position, velocity, drag_sum, weight_sum = lax.fori_loop(0, SUBSTEPS, substep, start_state)
    moved_state = jnp.concatenate([position, velocity], axis=1)
    nodal_sums = jnp.concatenate([drag_sum.reshape(batch_size, 3 * NODES), weight_sum], axis=1)
    return moved_state, nodal_sums


def local_update(field, viscosity, axial_speed, after_airway, before_airway, after_section, before_section):
    operator = jnp.asarray(operator_table(), dtype=jnp.float32)
    applied = jnp.einsum("mn,cnse->cmse", operator, field, precision=exact_mode)
    cube = field.reshape((3, 4, 4, 4) + field.shape[2:])
    faces = jnp.zeros_like(cube)
    faces = faces.at[:, 3].add(after_airway - cube[:, 3])
    faces = faces.at[:, 0].add(before_airway - cube[:, 0])
    faces = faces.at[:, :, 3].add(after_section - cube[:, :, 3])
    faces = faces.at[:, :, 0].add(before_section - cube[:, :, 0])
    return field + viscosity * applied[:, :NODES] - axial_speed * applied[:, NODES:] + penalty_weight * faces.reshape(field.shape)


def reference(fluid_velocity, viscosity, axial_speed, fluid_mass, positions, velocities, relax_rates, bin_element, bin_fill):
    occupancy = (jnp.arange(PER_BIN, dtype=jnp.int32)[None, :] < bin_fill[:, None]).astype(jnp.float32)
    records = jnp.concatenate([positions, velocities, relax_rates[:, None, :], occupancy[:, None, :]], axis=1)
    device_rank = jnp.arange(NB, dtype=jnp.int32) // BINS_CAP
    air_block = device_rank // N_SECTION
    sec_block = device_rank % N_SECTION
    global_element = ((sec_block * ES_DEV + bin_element // EA_DEV) * EA + air_block * EA_DEV + bin_element % EA_DEV).astype(jnp.int32)
    flat_fluid = fluid_velocity.reshape(3 * NODES, ES * EA)

    def one_block(pieces):
        block_records, block_element = pieces
        block_nodal = jnp.take(flat_fluid, block_element, axis=1).T
        return drag_bins(block_records, block_nodal)

    moved_state, nodal_sums = lax.map(one_block, (records.reshape(OVER, BINS_CAP, 8, PER_BIN), global_element.reshape(OVER, BINS_CAP)))
    particles_out = moved_state.reshape(NB, 6, PER_BIN)
    deposited = jax.ops.segment_sum(nodal_sums.reshape(NB, 4 * NODES), global_element, num_segments=ES * EA).T
    drag_part = deposited[:3 * NODES].reshape(3, NODES, ES, EA)
    weight_part = deposited[3 * NODES:].reshape(NODES, ES, EA)
    field = fluid_velocity - drag_part / (fluid_mass[None, None] + weight_part[None])
    for pass_index in range(PASSES):
        cube = field.reshape(3, 4, 4, 4, ES, EA)
        padded = jnp.pad(cube, ((0, 0), (0, 0), (0, 0), (0, 0), (1, 1), (1, 1)))
        field = local_update(field, viscosity, axial_speed, padded[:, 0, :, :, 1:-1, 2:], padded[:, 3, :, :, 1:-1, :-2], padded[:, :, 0, :, 2:, 1:-1], padded[:, :, 3, :, :-2, 1:-1])
    return field, particles_out
```

```python
import functools

import jax
import jax.numpy as jnp
import numpy as np
from jax import lax
from jax.experimental import pallas as pl
from jax.experimental.pallas import tpu as pltpu
from jax.sharding import PartitionSpec as P

NODES = 64
SUBSTEPS = 16
PASSES = 4
SUB = 8
LANE = 128
GROUPS_TOGETHER = 4

penalty_weight = 0.25
stride_step = 0.05
f32 = jnp.float32
bf16 = jnp.bfloat16


def iota(shape, dim):
    return lax.broadcasted_iota(jnp.int32, shape, dim)


def split(value):
    high = value.astype(bf16)
    low = (value - high.astype(f32)).astype(bf16)
    return high, low


def dot(a, b):
    return lax.dot_general(a, b, (((1,), (0,)), ((), ())), preferred_element_type=f32)


def dot_t(a, b):
    return lax.dot_general(a, b, (((1,), (1,)), ((), ())), preferred_element_type=f32)


def basis_values(x):
    square = x * x
    outer = 0.5625 * square - 0.0625
    inner = 1.6875 - 1.6875 * square
    outer_x = outer * x
    inner_x = inner * x
    third = inner * (1.0 / 3.0)
    return [outer - outer_x, third - inner_x, third + inner_x, outer + outer_x]


def send_faces(q, sa_next, sa_prev, ss_next, ss_prev):
    cells = q.shape[-1]
    lane = iota((SUB, LANE), 1)
    nxt = jnp.zeros((SUB, LANE), f32)
    prv = jnp.zeros((SUB, LANE), f32)
    for comp in range(3):
        for b in range(4):
            for c in range(4):
                i = comp * 16 + b * 4 + c
                tail = q[comp, 3, b, c, :, cells - LANE :]
                head = q[comp, 0, b, c, :, :LANE]
                nxt = jnp.where(lane == i, pltpu.roll(tail, (i + 1) % LANE, 1), nxt)
                prv = jnp.where(lane == i, pltpu.roll(head, i, 1), prv)
    sa_next[...] = nxt
    sa_prev[...] = prv
    for comp in range(3):
        for a in range(4):
            for c in range(4):
                i = a * 4 + c
                ss_next[comp, i : i + 1, :] = q[comp, a, 3, c, SUB - 1 : SUB, :]
                ss_prev[comp, i : i + 1, :] = q[comp, a, 0, c, 0:1, :]


def second_line(q, v_even, v_odd):
    even = v_even * ((q[0] + q[3]) - (q[1] + q[2]))
    odd = v_odd * ((q[3] - q[0]) - 3.0 * (q[2] - q[1]))
    third = odd * (1.0 / 3.0)
    return [even - odd, even - third, even + third, even + odd]


def pass_kernel(last, q, visc, speed, ha_after, ha_before, hs_after, hs_before, out, *sends):
    cells = q.shape[-1]
    tiles = cells // LANE
    lane = iota((SUB, LANE), 1)
    row = iota((SUB, LANE), 0)
    is_last_lane = lane == LANE - 1
    is_first_lane = lane == 0
    is_last_row = row == SUB - 1
    is_first_row = row == 0

    def component(comp, carry):
        halo_after = ha_after[...]
        halo_before = ha_before[...]
        for j in range(tiles):
            at = pl.ds(j * LANE, LANE)
            v_even = visc[:, at] * 1.125
            v_odd = visc[:, at] * 3.375
            s_even = speed[:, at] * 1.125
            s_odd = speed[:, at] * 1.125
            s_half = speed[:, at] * 0.5
            for b in range(4):
                plane = [[q[comp, a, b, c, :, at] for c in range(4)] for a in range(4)]
                along_c = [second_line(plane[a], v_even, v_odd) for a in range(4)]
                for c in range(4):
                    line = [plane[a][c] for a in range(4)]
                    rise = line[3] - line[0]
                    even = (line[0] + line[3]) - (line[1] + line[2])
                    odd = rise - 3.0 * (line[2] - line[1])
                    l_even = v_even * even
                    l_odd = v_odd * odd
                    l_third = l_odd * (1.0 / 3.0)
                    g_even = s_even * even
                    g_odd = s_odd * odd
                    g_rise = s_half * rise
                    g_even3 = g_even * (1.0 / 3.0)
                    g_outer = g_rise + g_odd
                    g_inner = g_rise - g_odd * (1.0 / 3.0)
                    new = [
                        (l_even + g_even) - (l_odd + g_outer),
                        (l_even + g_even3) - (l_third + g_inner),
                        (l_even - g_even3) + (l_third - g_inner),
                        (l_even - g_even) + (l_odd - g_outer),
                    ]
                    new = [line[a] + (new[a] + along_c[a][c]) for a in range(4)]
                    here = pltpu.roll(line[0], LANE - 1, 1)
                    if j == tiles - 1:
                        beyond = pltpu.roll(halo_after, (LANE - 1 - (comp * 16 + b * 4 + c)) % LANE, 1)
                    else:
                        beyond = pltpu.roll(q[comp, 0, b, c, :, pl.ds((j + 1) * LANE, LANE)], LANE - 1, 1)
                    after = jnp.where(is_last_lane, beyond, here)
                    here = pltpu.roll(line[3], 1, 1)
                    if j == 0:
                        beyond = pltpu.roll(halo_before, (LANE - (comp * 16 + b * 4 + c)) % LANE, 1)
                    else:
                        beyond = pltpu.roll(q[comp, 3, b, c, :, pl.ds((j - 1) * LANE, LANE)], 1, 1)
                    before = jnp.where(is_first_lane, beyond, here)
                    new[3] = new[3] + penalty_weight * (after - line[3])
                    new[0] = new[0] + penalty_weight * (before - line[0])
                    for a in range(4):
                        out[comp, a, b, c, :, at] = new[a]
            for a in range(4):
                for c in range(4):
                    line = [q[comp, a, b, c, :, at] for b in range(4)]
                    new = second_line(line, v_even, v_odd)
                    after = jnp.where(
                        is_last_row,
                        jnp.broadcast_to(hs_after[comp, a * 4 + c : a * 4 + c + 1, at], (SUB, LANE)),
                        pltpu.roll(line[0], SUB - 1, 0),
                    )
                    before = jnp.where(
                        is_first_row,
                        jnp.broadcast_to(hs_before[comp, a * 4 + c : a * 4 + c + 1, at], (SUB, LANE)),
                        pltpu.roll(line[3], 1, 0),
                    )
                    new[3] = new[3] + penalty_weight * (after - line[3])
                    new[0] = new[0] + penalty_weight * (before - line[0])
                    for b in range(4):
                        out[comp, a, b, c, :, at] = out[comp, a, b, c, :, at] + new[b]
        return carry

    lax.fori_loop(0, 3, component, 0)
    if not last:
        send_faces(out, *sends)


def particle_kernel(
    fluid,
    mass,
    positions,
    velocities,
    relax,
    element_row,
    fill_row,
    q_out,
    parts_out,
    sa_next,
    sa_prev,
    ss_next,
    ss_prev,
    state,
    rates,
    strides,
    occupied,
    nodal,
    sums,
    one_hot,
    rows_ref,
):
    bins = positions.shape[0]
    groups = bins // SUB
    lanes_bins = one_hot.shape[0]
    cells = fluid.shape[-1]
    row8 = iota((SUB, LANE), 0)
    lane8 = iota((SUB, LANE), 1)
    same = (lane8 % SUB == row8).astype(f32)

    rows_ref[...] = jnp.full(rows_ref.shape, -1.0, f32)
    rows_ref[0:1, :bins] = element_row[...].astype(f32)
    rows_ref[1:2, :bins] = fill_row[...].astype(f32)
    element_lanes = rows_ref[0:1, :]
    section_lanes = jnp.zeros_like(element_lanes)
    for s in range(1, SUB):
        section_lanes = section_lanes + (element_lanes >= float(s * cells)).astype(f32)

    lane_bins = iota((SUB, lanes_bins), 1)
    row_bins = iota((SUB, lanes_bins), 0)
    one_hot[...] = jnp.zeros(one_hot.shape, bf16)
    section_cols = []
    for g in range(groups):
        own = lane_bins == row_bins + g * SUB
        element = jnp.sum(jnp.where(own, element_lanes, 0.0), axis=1, keepdims=True)
        fill = jnp.sum(jnp.where(own, rows_ref[1:2, :], 0.0), axis=1, keepdims=True)
        section = jnp.zeros_like(element)
        for s in range(1, SUB):
            section = section + (element >= float(s * cells)).astype(f32)
        section_cols.append(section)
        column = element - section * float(cells)
        at = pl.ds(g * SUB, SUB)
        occ = (lane8.astype(f32) < fill).astype(f32)
        occupied[at, :] = occ
        rates[at, :] = relax[at, :] * occ
        strides[at, :] = occ * stride_step
        for k in range(3):
            state[k, at, :] = positions[at, k, :]
            state[3 + k, at, :] = velocities[at, k, :]
        hot = (iota((SUB, cells), 1).astype(f32) == column).astype(f32)
        one_hot[at, :] = hot.astype(bf16)

    spread = (iota((LANE, LANE), 0) // SUB == iota((LANE, LANE), 1) // SUB).astype(bf16)
    section_col = jnp.concatenate(section_cols, axis=0)
    in_section = (iota((bins, LANE), 1) % SUB).astype(f32) == section_col
    hot_bins = one_hot[:bins, :]
    for comp in range(3):
        for a in range(4):
            i = comp * 4 + a
            values = fluid[comp, a].reshape(16 * SUB, cells)
            for part, source in enumerate(split(values)):
                picked = jnp.where(in_section, dot_t(hot_bins, source), 0.0).astype(bf16)
                wide = dot(picked, spread)
                for g in range(groups):
                    block = (wide[g * SUB : (g + 1) * SUB, :] * same).astype(f32)
                    nodal[g, part, i * SUB : (i + 1) * SUB, :] = block.astype(bf16)

    sums[...] = jnp.zeros(sums.shape, f32)

    def substep(first, turn, carry):
        for g in range(first, first + GROUPS_TOGETHER):
            at = pl.ds(g * SUB, SUB)
            x = [state[k, at, :] for k in range(3)]
            v = [state[3 + k, at, :] for k in range(3)]
            rate = rates[at, :]
            step = strides[at, :]
            occ = occupied[at, :]
            la, lb, lc = [basis_values(x[k]) for k in range(3)]
            across = jnp.concatenate([lb[b] * lc[c] for b in range(4) for c in range(4)], axis=0)
            high, low = split(across)
            n_high = nodal[g, 0]
            n_low = nodal[g, 1]
            at_a = dot(n_high, high) + (dot(n_high, low) + dot(n_low, high))
            pushes = []
            for k in range(3):
                rows = [at_a[(k * 4 + a) * SUB : (k * 4 + a + 1) * SUB, :] for a in range(4)]
                u = (la[0] * rows[0] + la[1] * rows[1]) + (la[2] * rows[2] + la[3] * rows[3])
                dv = rate * (u - v[k])
                moved = v[k] + dv
                state[3 + k, at, :] = moved
                state[k, at, :] = jnp.clip(x[k] + step * moved, -1.0, 1.0)
                pushes += [la[a] * dv for a in range(4)]
            push_high, push_low = split(jnp.concatenate(pushes, axis=0))
            drag = dot_t(push_high, high) + (dot_t(push_high, low) + dot_t(push_low, high))
            square_high, square_low = split(across * across)
            weigh_high, weigh_low = split(
                jnp.concatenate([la[a] * la[a] * occ for a in range(4)], axis=0)
            )
            weight = dot_t(weigh_high, square_high) + (
                dot_t(weigh_high, square_low) + dot_t(weigh_low, square_high)
            )
            sums[g] = sums[g] + jnp.concatenate([drag, weight], axis=0)
        return carry

    for first in range(0, groups, GROUPS_TOGETHER):
        lax.fori_loop(0, SUBSTEPS, functools.partial(substep, first), 0)

    for g in range(groups):
        at = pl.ds(g * SUB, SUB)
        for k in range(6):
            parts_out[at, k, :] = state[k, at, :]

    in_section_rows = (iota((LANE, lanes_bins), 0) % SUB).astype(f32) == section_lanes
    hot_all = one_hot[...]
    spread2 = spread

    def deposit(i):
        blocks = [sums[g, i * SUB : (i + 1) * SUB, :] * same for g in range(groups)]
        blocks += [jnp.zeros((SUB, LANE), f32)] * (lanes_bins // SUB - groups)
        high, low = split(jnp.concatenate(blocks, axis=0))
        wide = dot_t(spread2, high) + dot_t(spread2, low)
        wide = jnp.where(in_section_rows, wide, 0.0)
        high, low = split(wide)
        return dot(high, hot_all) + dot(low, hot_all)

    for a in range(4):
        weight = deposit(12 + a).reshape(4, 4, SUB, cells)
        scale = 1.0 / (mass[...][None, None] + weight)
        for comp in range(3):
            drag = deposit(comp * 4 + a).reshape(4, 4, SUB, cells)
            q_out[comp, a] = fluid[comp, a] - drag * scale

    send_faces(q_out, sa_next, sa_prev, ss_next, ss_prev)


def shift(values, axis, up):
    count = lax.axis_size(axis)
    ends = count - 1
    if up:
        pairs = [(i, i + 1) for i in range(ends)]
    else:
        pairs = [(i + 1, i) for i in range(ends)]
    return lax.ppermute(values, axis, pairs)


def exchange(faces):
    sa_next, sa_prev, ss_next, ss_prev = faces
    ha_before = shift(sa_next, "airway", True)
    ha_after = shift(sa_prev, "airway", False)
    hs_before = shift(ss_next, "section", True)
    hs_after = shift(ss_prev, "section", False)
    return ha_after, ha_before, hs_after, hs_before


def local(
    fluid_velocity,
    viscosity,
    axial_speed,
    fluid_mass,
    positions,
    velocities,
    relax_rates,
    bin_element,
    bin_fill,
):
    sec_cells, air_cells = fluid_velocity.shape[2:]
    bins = positions.shape[0]
    groups = bins // SUB
    lanes_bins = -(-bins // LANE) * LANE
    field_shape = (3, 4, 4, 4, sec_cells, air_cells)
    field = jax.ShapeDtypeStruct(field_shape, f32)
    face_shapes = (
        jax.ShapeDtypeStruct((sec_cells, LANE), f32),
        jax.ShapeDtypeStruct((sec_cells, LANE), f32),
        jax.ShapeDtypeStruct((3, 16, air_cells), f32),
        jax.ShapeDtypeStruct((3, 16, air_cells), f32),
    )
    vmem = pl.BlockSpec(memory_space=pltpu.VMEM)
    params = pltpu.CompilerParams(vmem_limit_bytes=48 * 1024 * 1024)
    q, particles_out, *faces = pl.pallas_call(
        particle_kernel,
        out_shape=(field, jax.ShapeDtypeStruct((bins, 6, LANE), f32)) + face_shapes,
        in_specs=[vmem] * 7,
        out_specs=(vmem,) * 6,
        scratch_shapes=[
            pltpu.VMEM((6, bins, LANE), f32),
            pltpu.VMEM((bins, LANE), f32),
            pltpu.VMEM((bins, LANE), f32),
            pltpu.VMEM((bins, LANE), f32),
            pltpu.VMEM((groups, 2, 96, LANE), bf16),
            pltpu.VMEM((groups, LANE, LANE), f32),
            pltpu.VMEM((lanes_bins, air_cells), bf16),
            pltpu.VMEM((SUB, lanes_bins), f32),
        ],
        compiler_params=params,
        name="particles",
    )(
        fluid_velocity.reshape(field_shape),
        fluid_mass,
        positions,
        velocities,
        relax_rates,
        bin_element.reshape(1, bins),
        bin_fill.reshape(1, bins),
    )
    for turn in range(PASSES):
        last = turn == PASSES - 1
        halos = exchange(faces)
        q, *faces = pl.pallas_call(
            functools.partial(pass_kernel, last),
            out_shape=(field,) + (() if last else face_shapes),
            in_specs=[vmem] * 7,
            out_specs=(vmem,) * (1 if last else 5),
            compiler_params=params,
            name="advance",
        )(q, viscosity, axial_speed, *halos)
    return (q.reshape(3, NODES, sec_cells, air_cells), particles_out)


def solution(mesh):
    return jax.shard_map(
        local,
        mesh=mesh,
        in_specs=(
            P(None, None, "section", "airway"),
            P("section", "airway"),
            P("section", "airway"),
            P("section", "airway"),
            P(("airway", "section"), None, None),
            P(("airway", "section"), None, None),
            P(("airway", "section"), None),
            P(("airway", "section")),
            P(("airway", "section")),
        ),
        out_specs=(P(None, None, "section", "airway"), P(("airway", "section"), None, None)),
        check_vma=False,
    )
```

```python
import functools

import jax
import jax.numpy as jnp
import numpy as np
from jax import lax
from jax.experimental import pallas as pl
from jax.experimental.pallas import tpu as pltpu
from jax.sharding import PartitionSpec as P

NODES = 64
SUBSTEPS = 16
PASSES = 4
SUB = 8
LANE = 128
GROUPS_TOGETHER = 4

penalty_weight = 0.25
stride_step = 0.05
f32 = jnp.float32
bf16 = jnp.bfloat16


def iota(shape, dim):
    return lax.broadcasted_iota(jnp.int32, shape, dim)


def split(value):
    high = value.astype(bf16)
    low = (value - high.astype(f32)).astype(bf16)
    return high, low


def dot(a, b):
    return lax.dot_general(a, b, (((1,), (0,)), ((), ())), preferred_element_type=f32)


def dot_t(a, b):
    return lax.dot_general(a, b, (((1,), (1,)), ((), ())), preferred_element_type=f32)


def basis_values(x):
    square = x * x
    outer = 0.5625 * square - 0.0625
    inner = 1.6875 - 1.6875 * square
    outer_x = outer * x
    inner_x = inner * x
    third = inner * (1.0 / 3.0)
    return [outer - outer_x, third - inner_x, third + inner_x, outer + outer_x]


def is_even(axis):
    return lax.axis_index(axis) % 2 == 0


def send_faces(q, sa_first, sa_second, ss_first, ss_second):
    cells = q.shape[-1]
    lane = iota((SUB, LANE), 1)
    nxt = jnp.zeros((SUB, LANE), f32)
    prv = jnp.zeros((SUB, LANE), f32)
    for comp in range(3):
        for b in range(4):
            for c in range(4):
                i = comp * 16 + b * 4 + c
                tail = q[comp, 3, b, c, :, cells - LANE :]
                head = q[comp, 0, b, c, :, :LANE]
                nxt = jnp.where(lane == i, pltpu.roll(tail, (i + 1) % LANE, 1), nxt)
                prv = jnp.where(lane == i, pltpu.roll(head, i, 1), prv)
    even = is_even("airway")
    sa_first[...] = jnp.where(even, nxt, prv)
    sa_second[...] = jnp.where(even, prv, nxt)
    even = is_even("section")
    for comp in range(3):
        for a in range(4):
            for c in range(4):
                i = a * 4 + c
                tail = q[comp, a, 3, c, SUB - 1 : SUB, :]
                head = q[comp, a, 0, c, 0:1, :]
                ss_first[comp, i : i + 1, :] = jnp.where(even, tail, head)
                ss_second[comp, i : i + 1, :] = jnp.where(even, head, tail)


def second_line(q, v_even, v_odd):
    even = v_even * ((q[0] + q[3]) - (q[1] + q[2]))
    odd = v_odd * ((q[3] - q[0]) - 3.0 * (q[2] - q[1]))
    third = odd * (1.0 / 3.0)
    return [even - odd, even - third, even + third, even + odd]


def pass_kernel(last, q, visc, speed, ha_first, ha_second, hs_first, hs_second, out, *sends):
    cells = q.shape[-1]
    tiles = cells // LANE
    lane = iota((SUB, LANE), 1)
    row = iota((SUB, LANE), 0)
    is_last_lane = lane == LANE - 1
    is_first_lane = lane == 0
    is_last_row = row == SUB - 1
    is_first_row = row == 0

    def component(comp, carry):
        forward = is_even("airway")
        halo_after = jnp.where(forward, ha_first[...], ha_second[...])
        halo_before = jnp.where(forward, ha_second[...], ha_first[...])
        forward = is_even("section")
        for j in range(tiles):
            at = pl.ds(j * LANE, LANE)
            v_even = visc[:, at] * 1.125
            v_odd = visc[:, at] * 3.375
            s_even = speed[:, at] * 1.125
            s_odd = speed[:, at] * 1.125
            s_half = speed[:, at] * 0.5
            for b in range(4):
                plane = [[q[comp, a, b, c, :, at] for c in range(4)] for a in range(4)]
                along_c = [second_line(plane[a], v_even, v_odd) for a in range(4)]
                for c in range(4):
                    line = [plane[a][c] for a in range(4)]
                    rise = line[3] - line[0]
                    even = (line[0] + line[3]) - (line[1] + line[2])
                    odd = rise - 3.0 * (line[2] - line[1])
                    l_even = v_even * even
                    l_odd = v_odd * odd
                    l_third = l_odd * (1.0 / 3.0)
                    g_even = s_even * even
                    g_odd = s_odd * odd
                    g_rise = s_half * rise
                    g_even3 = g_even * (1.0 / 3.0)
                    g_outer = g_rise + g_odd
                    g_inner = g_rise - g_odd * (1.0 / 3.0)
                    new = [
                        (l_even + g_even) - (l_odd + g_outer),
                        (l_even + g_even3) - (l_third + g_inner),
                        (l_even - g_even3) + (l_third - g_inner),
                        (l_even - g_even) + (l_odd - g_outer),
                    ]
                    new = [line[a] + (new[a] + along_c[a][c]) for a in range(4)]
                    here = pltpu.roll(line[0], LANE - 1, 1)
                    if j == tiles - 1:
                        beyond = pltpu.roll(halo_after, (LANE - 1 - (comp * 16 + b * 4 + c)) % LANE, 1)
                    else:
                        beyond = pltpu.roll(q[comp, 0, b, c, :, pl.ds((j + 1) * LANE, LANE)], LANE - 1, 1)
                    after = jnp.where(is_last_lane, beyond, here)
                    here = pltpu.roll(line[3], 1, 1)
                    if j == 0:
                        beyond = pltpu.roll(halo_before, (LANE - (comp * 16 + b * 4 + c)) % LANE, 1)
                    else:
                        beyond = pltpu.roll(q[comp, 3, b, c, :, pl.ds((j - 1) * LANE, LANE)], 1, 1)
                    before = jnp.where(is_first_lane, beyond, here)
                    new[3] = new[3] + penalty_weight * (after - line[3])
                    new[0] = new[0] + penalty_weight * (before - line[0])
                    for a in range(4):
                        out[comp, a, b, c, :, at] = new[a]
            for a in range(4):
                for c in range(4):
                    line = [q[comp, a, b, c, :, at] for b in range(4)]
                    new = second_line(line, v_even, v_odd)
                    i = a * 4 + c
                    first = jnp.broadcast_to(hs_first[comp, i : i + 1, at], (SUB, LANE))
                    second = jnp.broadcast_to(hs_second[comp, i : i + 1, at], (SUB, LANE))
                    after = jnp.where(
                        is_last_row,
                        jnp.where(forward, first, second),
                        pltpu.roll(line[0], SUB - 1, 0),
                    )
                    before = jnp.where(
                        is_first_row,
                        jnp.where(forward, second, first),
                        pltpu.roll(line[3], 1, 0),
                    )
                    new[3] = new[3] + penalty_weight * (after - line[3])
                    new[0] = new[0] + penalty_weight * (before - line[0])
                    for b in range(4):
                        out[comp, a, b, c, :, at] = out[comp, a, b, c, :, at] + new[b]
        return carry

    lax.fori_loop(0, 3, component, 0)
    if not last:
        send_faces(out, *sends)


def particle_kernel(
    fluid_hbm,
    mass_hbm,
    positions,
    velocities,
    relax_hbm,
    element_hbm,
    fill_hbm,
    q_out,
    parts_out,
    sa_first,
    sa_second,
    ss_first,
    ss_second,
    rates,
    strides,
    occupied,
    nodal,
    sums,
    totals,
    one_hot,
    rows_ref,
    fluid,
    mass,
    relax,
    element_row,
    fill_row,
    arrived,
):
    copies = [
        pltpu.make_async_copy(source, target, arrived.at[i])
        for i, (source, target) in enumerate(
            (
                (element_hbm, element_row),
                (fill_hbm, fill_row),
                (fluid_hbm, fluid),
                (relax_hbm, relax),
                (positions, parts_out.at[0:3]),
                (velocities, parts_out.at[3:6]),
                (mass_hbm, mass),
            )
        )
    ]
    for copy in copies:
        copy.start()
    bins = positions.shape[1]
    groups = bins // SUB
    lanes_bins = one_hot.shape[0]
    cells = fluid.shape[-1]
    row8 = iota((SUB, LANE), 0)
    lane8 = iota((SUB, LANE), 1)
    same = (lane8 % SUB == row8).astype(f32)

    copies[0].wait()
    copies[1].wait()

    rows_ref[...] = jnp.full(rows_ref.shape, -1.0, f32)
    rows_ref[0:1, :bins] = element_row[...].astype(f32)
    rows_ref[1:2, :bins] = fill_row[...].astype(f32)
    element_lanes = rows_ref[0:1, :]
    section_lanes = jnp.zeros_like(element_lanes)
    for s in range(1, SUB):
        section_lanes = section_lanes + (element_lanes >= float(s * cells)).astype(f32)

    lane_bins = iota((SUB, lanes_bins), 1)
    row_bins = iota((SUB, lanes_bins), 0)
    one_hot[...] = jnp.zeros(one_hot.shape, bf16)
    section_cols = []
    for g in range(groups):
        own = lane_bins == row_bins + g * SUB
        element = jnp.sum(jnp.where(own, element_lanes, 0.0), axis=1, keepdims=True)
        fill = jnp.sum(jnp.where(own, rows_ref[1:2, :], 0.0), axis=1, keepdims=True)
        section = jnp.zeros_like(element)
        for s in range(1, SUB):
            section = section + (element >= float(s * cells)).astype(f32)
        section_cols.append(section)
        column = element - section * float(cells)
        at = pl.ds(g * SUB, SUB)
        occ = (lane8.astype(f32) < fill).astype(f32)
        occupied[at, :] = occ
        strides[at, :] = occ * stride_step
        hot = (iota((SUB, cells), 1).astype(f32) == column).astype(f32)
        one_hot[at, :] = hot.astype(bf16)

    copies[2].wait()

    spread = (iota((LANE, LANE), 0) // SUB == iota((LANE, LANE), 1) // SUB).astype(bf16)
    section_col = jnp.concatenate(section_cols, axis=0)
    in_section = (iota((bins, LANE), 1) % SUB).astype(f32) == section_col
    hot_bins = one_hot[:bins, :]
    for comp in range(3):
        for a in range(4):
            i = comp * 4 + a
            values = fluid[comp, a].reshape(16 * SUB, cells)
            for part, source in enumerate(split(values)):
                picked = jnp.where(in_section, dot_t(hot_bins, source), 0.0).astype(bf16)
                wide = dot(picked, spread)
                for g in range(groups):
                    block = wide[g * SUB : (g + 1) * SUB, :] * same
                    nodal[g, part * 96 + i * SUB : part * 96 + (i + 1) * SUB, :] = block.astype(bf16)

    for copy in copies[3:]:
        copy.wait()
    rates[...] = relax[...] * occupied[...]
    totals[...] = jnp.zeros(totals.shape, f32)

    def substep(first, turn, carry):
        for slot in range(GROUPS_TOGETHER):
            g = first + slot
            at = pl.ds(g * SUB, SUB)
            x = [parts_out[k, at, :] for k in range(3)]
            v = [parts_out[3 + k, at, :] for k in range(3)]
            rate = rates[at, :]
            step = strides[at, :]
            occ = occupied[at, :]
            la, lb, lc = [basis_values(x[k]) for k in range(3)]
            across = [lb[b] * lc[c] for b in range(4) for c in range(4)]
            high, low = split(jnp.concatenate(across, axis=0))
            by_high = dot(nodal[g], high)
            at_a = by_high[:96] + (by_high[96:] + dot(nodal[g, :96], low))
            pushes = []
            for k in range(3):
                rows = [at_a[(k * 4 + a) * SUB : (k * 4 + a + 1) * SUB, :] for a in range(4)]
                u = (la[0] * rows[0] + la[1] * rows[1]) + (la[2] * rows[2] + la[3] * rows[3])
                dv = rate * (u - v[k])
                moved = v[k] + dv
                parts_out[3 + k, at, :] = moved
                parts_out[k, at, :] = jnp.clip(x[k] + step * moved, -1.0, 1.0)
                pushes += [la[a] * dv for a in range(4)]
            weighs = [la[a] * la[a] * occ for a in range(4)]
            for n in range(16):
                for i in range(12):
                    j = i * 16 + n
                    sums[slot, j] = sums[slot, j] + across[n] * pushes[i]
            for n in range(16):
                square = across[n] * across[n]
                for a in range(4):
                    j = (12 + a) * 16 + n
                    sums[slot, j] = sums[slot, j] + square * weighs[a]
        return carry

    def over_lanes(slot, start):
        terms = [sums[slot, start + n] for n in range(LANE)]
        width = 1
        while width < LANE:
            upper = (lane8 // width) % 2 == 1
            terms = [
                jnp.where(upper, odd, even) + pltpu.roll(jnp.where(upper, even, odd), width, 1)
                for even, odd in zip(terms[0::2], terms[1::2])
            ]
            width *= 2
        return terms[0]

    for first in range(0, groups, GROUPS_TOGETHER):
        sums[...] = jnp.zeros(sums.shape, f32)
        lax.fori_loop(0, SUBSTEPS, functools.partial(substep, first), 0)
        for slot in range(GROUPS_TOGETHER):
            at = pl.ds((first + slot) * SUB, SUB)
            totals[at, :LANE] = over_lanes(slot, 0)
            totals[at, LANE:] = over_lanes(slot, LANE)

    in_section_rows = (iota((LANE, lanes_bins), 0) % SUB).astype(f32) == section_lanes
    hot_all = one_hot[...]
    spread_rows = (iota((LANE, 16), 0) // SUB == iota((LANE, 16), 1)).astype(bf16)
    by_node = jnp.concatenate([totals[:, :LANE].T, totals[:, LANE:].T], axis=0)

    for a in range(4):
        highs = []
        lows = []
        for i in (12 + a, a, 4 + a, 8 + a):
            high, low = split(by_node[i * 16 : (i + 1) * 16, :])
            wide = dot(spread_rows, high) + dot(spread_rows, low)
            high, low = split(jnp.where(in_section_rows, wide, 0.0))
            highs.append(high)
            lows.append(low)
        placed = dot(jnp.concatenate(highs + lows, axis=0), hot_all)
        placed = (placed[: 4 * LANE] + placed[4 * LANE :]).reshape(4, 4, 4, SUB, cells)
        scale = 1.0 / (mass[...][None, None] + placed[0])
        for comp in range(3):
            q_out[comp, a] = fluid[comp, a] - placed[1 + comp] * scale

    send_faces(q_out, sa_first, sa_second, ss_first, ss_second)


def swap(values, axis, offset):
    count = lax.axis_size(axis)
    pairs = []
    for i in range(offset, count - 1, 2):
        pairs += [(i, i + 1), (i + 1, i)]
    return lax.ppermute(values, axis, pairs)


def exchange(faces):
    sa_first, sa_second, ss_first, ss_second = faces
    return (
        swap(sa_first, "airway", 0),
        swap(sa_second, "airway", 1),
        swap(ss_first, "section", 0),
        swap(ss_second, "section", 1),
    )


def local(
    fluid_velocity,
    viscosity,
    axial_speed,
    fluid_mass,
    positions,
    velocities,
    relax_rates,
    bin_element,
    bin_fill,
):
    sec_cells, air_cells = fluid_velocity.shape[2:]
    bins = positions.shape[0]
    groups = bins // SUB
    lanes_bins = -(-bins // LANE) * LANE
    field_shape = (3, 4, 4, 4, sec_cells, air_cells)
    field = jax.ShapeDtypeStruct(field_shape, f32)
    face_shapes = (
        jax.ShapeDtypeStruct((sec_cells, LANE), f32),
        jax.ShapeDtypeStruct((sec_cells, LANE), f32),
        jax.ShapeDtypeStruct((3, 16, air_cells), f32),
        jax.ShapeDtypeStruct((3, 16, air_cells), f32),
    )
    vmem = pl.BlockSpec(memory_space=pltpu.VMEM)
    hbm = pl.BlockSpec(memory_space=pltpu.HBM)
    params = pltpu.CompilerParams(vmem_limit_bytes=48 * 1024 * 1024)
    q, particles_out, *faces = pl.pallas_call(
        particle_kernel,
        out_shape=(field, jax.ShapeDtypeStruct((6, bins, LANE), f32)) + face_shapes,
        in_specs=[hbm] * 7,
        out_specs=(vmem,) * 6,
        scratch_shapes=[
            pltpu.VMEM((bins, LANE), f32),
            pltpu.VMEM((bins, LANE), f32),
            pltpu.VMEM((bins, LANE), f32),
            pltpu.VMEM((groups, 192, LANE), bf16),
            pltpu.VMEM((GROUPS_TOGETHER, 256, SUB, LANE), f32),
            pltpu.VMEM((lanes_bins, 256), f32),
            pltpu.VMEM((lanes_bins, air_cells), bf16),
            pltpu.VMEM((SUB, lanes_bins), f32),
            pltpu.VMEM(field_shape, f32),
            pltpu.VMEM(fluid_mass.shape, f32),
            pltpu.VMEM(relax_rates.shape, f32),
            pltpu.VMEM((1, bins), jnp.int32),
            pltpu.VMEM((1, bins), jnp.int32),
            pltpu.SemaphoreType.DMA((7,)),
        ],
        compiler_params=params,
        name="particles",
    )(
        *(
            pltpu.with_memory_space_constraint(array, pltpu.HBM)
            for array in (
                fluid_velocity.reshape(field_shape),
                fluid_mass,
                positions.transpose(1, 0, 2),
                velocities.transpose(1, 0, 2),
                relax_rates,
                bin_element.reshape(1, bins),
                bin_fill.reshape(1, bins),
            )
        )
    )
    for turn in range(PASSES):
        last = turn == PASSES - 1
        halos = exchange(faces)
        q, *faces = pl.pallas_call(
            functools.partial(pass_kernel, last),
            out_shape=(field,) + (() if last else face_shapes),
            in_specs=[vmem] * 7,
            out_specs=(vmem,) * (1 if last else 5),
            compiler_params=params,
            name="advance",
        )(q, viscosity, axial_speed, *halos)
    return (q.reshape(3, NODES, sec_cells, air_cells), particles_out.transpose(1, 0, 2))


def solution(mesh):
    return jax.shard_map(
        local,
        mesh=mesh,
        in_specs=(
            P(None, None, "section", "airway"),
            P("section", "airway"),
            P("section", "airway"),
            P("section", "airway"),
            P(("airway", "section"), None, None),
            P(("airway", "section"), None, None),
            P(("airway", "section"), None),
            P(("airway", "section")),
            P(("airway", "section")),
        ),
        out_specs=(P(None, None, "section", "airway"), P(("airway", "section"), None, None)),
        check_vma=False,
    )
```

```python
import functools

import jax
import jax.numpy as jnp
import numpy as np
from jax import lax
from jax.experimental import pallas as pl
from jax.experimental.pallas import tpu as pltpu
from jax.sharding import PartitionSpec as P

NODES = 64
SUBSTEPS = 16
PASSES = 4
SUB = 8
LANE = 128
GROUPS_TOGETHER = 4

penalty_weight = 0.25
stride_step = 0.05
f32 = jnp.float32
bf16 = jnp.bfloat16


def iota(shape, dim):
    return lax.broadcasted_iota(jnp.int32, shape, dim)


def split(value):
    high = value.astype(bf16)
    low = (value - high.astype(f32)).astype(bf16)
    return high, low


def dot(a, b):
    return lax.dot_general(a, b, (((1,), (0,)), ((), ())), preferred_element_type=f32)


def dot_t(a, b):
    return lax.dot_general(a, b, (((1,), (1,)), ((), ())), preferred_element_type=f32)


def basis_values(x):
    square = x * x
    outer = 0.5625 * square - 0.0625
    inner = 1.6875 - 1.6875 * square
    outer_x = outer * x
    inner_x = inner * x
    third = inner * (1.0 / 3.0)
    return [outer - outer_x, third - inner_x, third + inner_x, outer + outer_x]


def is_even(axis):
    return lax.axis_index(axis) % 2 == 0


def pack_columns(q, visc, speed, first, second):
    cells = q.shape[-1]
    lane = iota((SUB, LANE), 1)
    even = is_even("airway")
    for tile in range(9):
        nxt = jnp.zeros((SUB, LANE), f32)
        prv = jnp.zeros((SUB, LANE), f32)
        for n in range(tile * 8, min(tile * 8 + 8, 66)):
            for comp in range(3):
                if n < NODES:
                    tail = q[comp, n // 16, n // 4 % 4, n % 4, :, cells - LANE :]
                    head = q[comp, n // 16, n // 4 % 4, n % 4, :, :LANE]
                else:
                    source = visc if n == NODES else speed
                    tail = source[:, cells - LANE :]
                    head = source[:, :LANE]
                start = 64 * (n // 4 % 2) + 16 * comp + 4 * (n % 4)
                here = (lane >= start) & (lane < start + 4)
                nxt = jnp.where(here, pltpu.roll(tail, (start + 4) % LANE, 1), nxt)
                prv = jnp.where(here, pltpu.roll(head, start, 1), prv)
        first[tile] = jnp.where(even, nxt, prv)
        second[tile] = jnp.where(even, prv, nxt)


def second_line(q, v_even, v_odd):
    even = v_even * ((q[0] + q[3]) - (q[1] + q[2]))
    odd = v_odd * ((q[3] - q[0]) - 3.0 * (q[2] - q[1]))
    third = odd * (1.0 / 3.0)
    return [even - odd, even - third, even + third, even + odd]


def advance_tile(
    load, store, v, g, beyond_next, beyond_prev, row_after, row_before, valid=None, drive=None
):
    lane = iota((SUB, LANE), 1)
    v_even, v_odd = v * 1.125, v * 3.375
    s_even, s_half = g * 1.125, g * 0.5
    for b in range(4):
        plane = [[load(a, b, c) for c in range(4)] for a in range(4)]
        along_c = [second_line(plane[a], v_even, v_odd) for a in range(4)]
        for c in range(4):
            line = [plane[a][c] for a in range(4)]
            rise = line[3] - line[0]
            even = (line[0] + line[3]) - (line[1] + line[2])
            odd = rise - 3.0 * (line[2] - line[1])
            l_even = v_even * even
            l_odd = v_odd * odd
            l_third = l_odd * (1.0 / 3.0)
            g_even = s_even * even
            g_odd = s_even * odd
            g_rise = s_half * rise
            g_even3 = g_even * (1.0 / 3.0)
            g_outer = g_rise + g_odd
            g_inner = g_rise - g_odd * (1.0 / 3.0)
            new = [
                (l_even + g_even) - (l_odd + g_outer),
                (l_even + g_even3) - (l_third + g_inner),
                (l_even - g_even3) + (l_third - g_inner),
                (l_even - g_even) + (l_odd - g_outer),
            ]
            new = [line[a] + (new[a] + along_c[a][c]) for a in range(4)]
            after = pltpu.roll(line[0], LANE - 1, 1)
            if beyond_next is not None:
                after = jnp.where(lane == LANE - 1, pltpu.roll(beyond_next(0, b, c), LANE - 1, 1), after)
            before = pltpu.roll(line[3], 1, 1)
            if beyond_prev is not None:
                before = jnp.where(lane == 0, pltpu.roll(beyond_prev(3, b, c), 1, 1), before)
            new[3] = new[3] + penalty_weight * (after - line[3])
            new[0] = new[0] + penalty_weight * (before - line[0])
            for a in range(4):
                store(a, b, c, new[a])
    return v_even, v_odd


def advance_rows(
    load, partial, store, v, row_after, row_before, valid=None, drive=None
):
    v_even, v_odd = v * 1.125, v * 3.375
    for a in range(4):
        for c in range(4):
            line = [load(a, b, c) for b in range(4)]
            new = second_line(line, v_even, v_odd)
            after = jnp.where(row_after, pltpu.roll(line[0], SUB - 1, 0), 0.0)
            before = jnp.where(row_before, pltpu.roll(line[3], 1, 0), 0.0)
            if drive is not None:
                more_after, more_before = drive(a * 4 + c)
                after = after + more_after
                before = before + more_before
            new[3] = new[3] + penalty_weight * (after - line[3])
            new[0] = new[0] + penalty_weight * (before - line[0])
            for b in range(4):
                value = partial(a, b, c) + new[b]
                store(a, b, c, value if valid is None else value * valid)


def advance_main(source, target, visc, speed, row_after, row_before, drive=None):
    tiles = source.shape[-1] // LANE

    def component(comp, carry):
        for j in range(tiles):
            at = pl.ds(j * LANE, LANE)
            at_next = pl.ds((j + 1) % tiles * LANE, LANE)
            at_prev = pl.ds((j - 1) % tiles * LANE, LANE)

            def load(a, b, c):
                return source[comp, a, b, c, :, at]

            def store(a, b, c, value):
                target[comp, a, b, c, :, at] = value

            v = visc[:, at]
            advance_tile(
                load,
                store,
                v,
                speed[:, at],
                lambda a, b, c: source[comp, a, b, c, :, at_next],
                lambda a, b, c: source[comp, a, b, c, :, at_prev],
                row_after,
                row_before,
            )
            advance_rows(
                load,
                lambda a, b, c: target[comp, a, b, c, :, at],
                store,
                v,
                row_after,
                row_before,
                drive=None if drive is None else functools.partial(drive, comp, at),
            )
        return carry

    lax.fori_loop(0, 3, component, 0)


def advance_strip(source, target, v, g, valid, row_after, row_before, drive=None):
    def load(a, b, c):
        return source[a, b, c]

    def store(a, b, c, value):
        target[a, b, c] = value

    advance_tile(load, store, v, g, None, None, row_after, row_before)
    advance_rows(
        load,
        lambda a, b, c: target[a, b, c],
        store,
        v,
        row_after,
        row_before,
        valid=valid,
        drive=drive,
    )


FACE_BLOCKS = PASSES * 3 * 2
STRIP_BLOCKS = PASSES
COEFFICIENTS = FACE_BLOCKS + STRIP_BLOCKS


def face_row(faces, turn, comp, i, at):
    return faces[(turn * 3 + comp) * 2 + i // SUB, i % SUB : i % SUB + 1, at]


def strip_at(turn, i):
    block = FACE_BLOCKS + turn // 2 * 2 + i // SUB
    return block, i % SUB, pl.ds(turn % 2 * LANE, LANE)


def block_rows():
    row = iota((SUB, LANE), 0)
    return row != SUB - 1, row != 0


def strip_valid():
    lane = iota((SUB, LANE), 1)
    place = lane % 16
    index = lax.axis_index("airway")
    first = (index == 0).astype(f32)
    last = (index == lax.axis_size("airway") - 1).astype(f32)
    left = ((lane < 64) & (place < 4)).astype(f32)
    right = ((lane >= 64) & (place >= 8)).astype(f32)
    return 1.0 - left * first - right * last


def main_kernel(q, visc, speed, out, faces_first, faces_second, spare):
    row_after, row_before = block_rows()
    even = is_even("section")

    def pack(source, turn):
        for comp in range(3):
            for i in range(16):
                tail = source[comp, i // 4, 3, i % 4, SUB - 1 : SUB, :]
                head = source[comp, i // 4, 0, i % 4, 0:1, :]
                block = (turn * 3 + comp) * 2 + i // SUB
                at = pl.ds(i % SUB, 1)
                faces_first[block, at, :] = jnp.where(even, tail, head)
                faces_second[block, at, :] = jnp.where(even, head, tail)

    pack(q, 0)
    advance_main(q, out, visc, speed, row_after, row_before)
    pack(out, 1)
    advance_main(out, spare, visc, speed, row_after, row_before)
    pack(spare, 2)
    advance_main(spare, out, visc, speed, row_after, row_before)
    pack(out, 3)


def strip_kernel(
    q,
    visc,
    speed,
    air_first,
    air_second,
    faces_first,
    faces_second,
    out,
    strip_v,
    strip_g,
    sent_first,
    sent_second,
    spare,
):
    cells = q.shape[-1]
    lane = iota((SUB, LANE), 1)
    place = lane % 16
    forward = is_even("airway")
    left = (lane < 64) & (place < 4)
    right = (lane >= 64) & (place >= 8)

    def assemble(n, heads, tails):
        total = jnp.zeros((SUB, LANE), f32)
        for comp in range(3):
            base = 16 * comp
            total = jnp.where(lane // 16 == comp, pltpu.roll(heads[comp], base + 4, 1), total)
            total = jnp.where(
                lane // 16 == comp + 4, pltpu.roll(tails[comp], (base + 72) % LANE, 1), total
            )
        one = air_first[n // 8]
        two = air_second[n // 8]
        offset = 64 * (n // 4 % 2) + 4 * (n % 4)
        from_next = jnp.where(forward, one, two)
        from_prev = jnp.where(forward, two, one)
        total = jnp.where(left, pltpu.roll(from_prev, (LANE - offset) % LANE, 1), total)
        total = jnp.where(right, pltpu.roll(from_next, (LANE + 72 - offset) % LANE, 1), total)
        return jnp.where(place < 12, total, 0.0)

    for n in range(NODES):
        a, b, c = n // 16, n // 4 % 4, n % 4
        out[a, b, c] = assemble(
            n,
            [q[k, a, b, c, :, :LANE] for k in range(3)],
            [q[k, a, b, c, :, cells - LANE :] for k in range(3)],
        )
    strip_v[...] = assemble(NODES, [visc[:, :LANE]] * 3, [visc[:, cells - LANE :]] * 3)
    strip_g[...] = assemble(NODES + 1, [speed[:, :LANE]] * 3, [speed[:, cells - LANE :]] * 3)

    row_after, row_before = block_rows()
    even = is_even("section")
    sent_first[:FACE_BLOCKS] = faces_first[...]
    sent_second[:FACE_BLOCKS] = faces_second[...]

    def send(block, row, at, tail, head):
        sent_first[block, row : row + 1, at] = jnp.where(even, tail, head)
        sent_second[block, row : row + 1, at] = jnp.where(even, head, tail)

    def pack(source, turn):
        for i in range(16):
            block, row, at = strip_at(turn, i)
            send(
                block,
                row,
                at,
                source[i // 4, 3, i % 4, SUB - 1 : SUB, :],
                source[i // 4, 0, i % 4, 0:1, :],
            )

    everything = pl.ds(0, cells)
    sent_first[COEFFICIENTS] = jnp.zeros((SUB, cells), f32)
    sent_second[COEFFICIENTS] = jnp.zeros((SUB, cells), f32)
    send(COEFFICIENTS, 0, everything, visc[SUB - 1 : SUB, :], visc[0:1, :])
    send(COEFFICIENTS, 1, everything, speed[SUB - 1 : SUB, :], speed[0:1, :])
    send(COEFFICIENTS, 2, pl.ds(0, LANE), strip_v[SUB - 1 : SUB, :], strip_v[0:1, :])
    send(COEFFICIENTS, 2, pl.ds(LANE, LANE), strip_g[SUB - 1 : SUB, :], strip_g[0:1, :])

    v, g, valid = strip_v[...], strip_g[...], strip_valid()
    pack(out, 0)
    advance_strip(out, spare, v, g, valid, row_after, row_before)
    pack(spare, 1)
    advance_strip(spare, out, v, g, valid, row_after, row_before)
    pack(out, 2)
    advance_strip(out, spare, v, g, valid, row_after, row_before)
    pack(spare, 3)
    out[...] = spare[...]


def fourth_kernel(w, strip, visc, speed, strip_v, strip_g, w_out, strip_out):
    row_after, row_before = block_rows()
    advance_main(w, w_out, visc, speed, row_after, row_before)
    advance_strip(
        strip, strip_out, strip_v[...], strip_g[...], strip_valid(), row_after, row_before
    )


def edge_kernel(
    w,
    strip,
    visc,
    speed,
    strip_v,
    strip_g,
    sent_first,
    sent_second,
    got_first,
    got_second,
    out,
    e_one,
    e_two,
    z_one,
    z_two,
    e_visc,
    e_speed,
):
    cells = w.shape[-1]
    tiles = cells // LANE
    row = iota((SUB, LANE), 0)
    lane = iota((SUB, LANE), 1)
    even = is_even("section")
    index = lax.axis_index("section")
    has_prev = index > 0
    has_next = index < lax.axis_size("section") - 1
    row_after = (row != SUB - 1) & ((row != 0) | has_prev)
    row_before = (row != 0) & ((row != SUB - 1) | has_next)

    def rows_of(own, prev_row, next_row):
        moved = jnp.where(row == 1, pltpu.roll(own, 1, 0), 0.0)
        moved = jnp.where(row == 2, pltpu.roll(own, 1, 0), moved)
        moved = jnp.where((row == 5) | (row == 6), pltpu.roll(own, SUB - 1, 0), moved)
        moved = jnp.where(row == 0, jnp.broadcast_to(prev_row, (SUB, LANE)), moved)
        return jnp.where(row == SUB - 1, jnp.broadcast_to(next_row, (SUB, LANE)), moved)

    def received(block, r, at):
        one = got_first[block, r : r + 1, at]
        two = got_second[block, r : r + 1, at]
        return jnp.where(even, two, one), jnp.where(even, one, two)

    for j in range(tiles):
        at = pl.ds(j * LANE, LANE)
        e_visc[:, at] = rows_of(visc[:, at], *received(COEFFICIENTS, 0, at))
        e_speed[:, at] = rows_of(speed[:, at], *received(COEFFICIENTS, 1, at))
    z_v = rows_of(strip_v[...], *received(COEFFICIENTS, 2, pl.ds(0, LANE)))
    z_g = rows_of(strip_g[...], *received(COEFFICIENTS, 2, pl.ds(LANE, LANE)))
    valid = strip_valid()

    def forcing(pick):
        one = jnp.broadcast_to(pick(got_first), (SUB, LANE))
        two = jnp.broadcast_to(pick(got_second), (SUB, LANE))
        own_one = jnp.broadcast_to(pick(sent_first), (SUB, LANE))
        own_two = jnp.broadcast_to(pick(sent_second), (SUB, LANE))
        from_next = jnp.where(even, one, two)
        from_prev = jnp.where(even, two, one)
        own_next = jnp.where(even, own_one, own_two)
        own_prev = jnp.where(even, own_two, own_one)
        after = jnp.where(
            row == 6, from_next, jnp.where((row == 0) & has_prev, own_prev, 0.0)
        )
        before = jnp.where(
            row == 1, from_prev, jnp.where((row == SUB - 1) & has_next, own_next, 0.0)
        )
        return after, before

    def drive(turn, comp, at, i):
        return forcing(lambda faces: face_row(faces, turn, comp, i, at))

    def drive_strip(turn, i):
        block, r, at = strip_at(turn, i)
        return forcing(lambda faces: faces[block, r : r + 1, at])

    def first_component(comp, carry):
        for j in range(tiles):
            at = pl.ds(j * LANE, LANE)
            for i in range(16):
                a, c = i // 4, i % 4
                after, before = drive(0, comp, at, i)
                e_one[comp, a, 3, c, :, at] = penalty_weight * after
                e_one[comp, a, 0, c, :, at] = penalty_weight * before
                for b in (1, 2):
                    e_one[comp, a, b, c, :, at] = jnp.zeros((SUB, LANE), f32)
        return carry

    lax.fori_loop(0, 3, first_component, 0)
    for i in range(16):
        a, c = i // 4, i % 4
        after, before = drive_strip(0, i)
        z_one[a, 3, c] = penalty_weight * after * valid
        z_one[a, 0, c] = penalty_weight * before * valid
        for b in (1, 2):
            z_one[a, b, c] = jnp.zeros((SUB, LANE), f32)

    for turn, (source, target, z_source, z_target) in enumerate(
        ((e_one, e_two, z_one, z_two), (e_two, e_one, z_two, z_one), (e_one, e_two, z_one, z_two)),
        1,
    ):
        advance_main(
            source,
            target,
            e_visc,
            e_speed,
            row_after,
            row_before,
            functools.partial(drive, turn),
        )
        advance_strip(
            z_source,
            z_target,
            z_v,
            z_g,
            valid,
            row_after,
            row_before,
            functools.partial(drive_strip, turn),
        )

    low = row < 2
    high = row >= 6

    def back(effect):
        return jnp.where(
            low, pltpu.roll(effect, SUB - 1, 0), jnp.where(high, pltpu.roll(effect, 1, 0), 0.0)
        )

    for n in range(NODES):
        a, b, c = n // 16, n // 4 % 4, n % 4
        z_one[a, b, c] = strip[a, b, c] + back(z_two[a, b, c])

    def finish(comp, carry):
        for n in range(NODES):
            a, b, c = n // 16, n // 4 % 4, n % 4
            edge = z_one[a, b, c]
            for j in range(tiles):
                at = pl.ds(j * LANE, LANE)
                value = w[comp, a, b, c, :, at] + back(e_two[comp, a, b, c, :, at])
                if j == 0:
                    value = jnp.where(lane < 4, pltpu.roll(edge, LANE - 4 - 16 * comp, 1), value)
                if j == tiles - 1:
                    value = jnp.where(
                        lane >= LANE - 4, pltpu.roll(edge, LANE - 4 - 68 - 16 * comp, 1), value
                    )
                out[comp, a, b, c, :, at] = value
        return carry

    lax.fori_loop(0, 3, finish, 0)


def particle_kernel(
    fluid_hbm,
    mass_hbm,
    positions,
    velocities,
    relax_hbm,
    element_hbm,
    fill_hbm,
    visc_hbm,
    speed_hbm,
    q_out,
    parts_out,
    air_first,
    air_second,
    rates,
    strides,
    occupied,
    nodal,
    sums,
    totals,
    one_hot,
    rows_ref,
    fluid,
    mass,
    relax,
    element_row,
    fill_row,
    visc,
    speed,
    arrived,
):
    copies = [
        pltpu.make_async_copy(source, target, arrived.at[i])
        for i, (source, target) in enumerate(
            (
                (element_hbm, element_row),
                (fill_hbm, fill_row),
                (fluid_hbm, fluid),
                (relax_hbm, relax),
                (positions, parts_out.at[0:3]),
                (velocities, parts_out.at[3:6]),
                (mass_hbm, mass),
                (visc_hbm, visc),
                (speed_hbm, speed),
            )
        )
    ]
    for copy in copies:
        copy.start()
    bins = positions.shape[1]
    groups = bins // SUB
    lanes_bins = one_hot.shape[0]
    cells = fluid.shape[-1]
    row8 = iota((SUB, LANE), 0)
    lane8 = iota((SUB, LANE), 1)
    same = (lane8 % SUB == row8).astype(f32)

    copies[0].wait()
    copies[1].wait()

    rows_ref[...] = jnp.full(rows_ref.shape, -1.0, f32)
    rows_ref[0:1, :bins] = element_row[...].astype(f32)
    rows_ref[1:2, :bins] = fill_row[...].astype(f32)
    element_lanes = rows_ref[0:1, :]
    section_lanes = jnp.zeros_like(element_lanes)
    for s in range(1, SUB):
        section_lanes = section_lanes + (element_lanes >= float(s * cells)).astype(f32)

    lane_bins = iota((SUB, lanes_bins), 1)
    row_bins = iota((SUB, lanes_bins), 0)
    one_hot[...] = jnp.zeros(one_hot.shape, bf16)
    section_cols = []
    for g in range(groups):
        own = lane_bins == row_bins + g * SUB
        element = jnp.sum(jnp.where(own, element_lanes, 0.0), axis=1, keepdims=True)
        fill = jnp.sum(jnp.where(own, rows_ref[1:2, :], 0.0), axis=1, keepdims=True)
        section = jnp.zeros_like(element)
        for s in range(1, SUB):
            section = section + (element >= float(s * cells)).astype(f32)
        section_cols.append(section)
        column = element - section * float(cells)
        at = pl.ds(g * SUB, SUB)
        occ = (lane8.astype(f32) < fill).astype(f32)
        occupied[at, :] = occ
        strides[at, :] = occ * stride_step
        hot = (iota((SUB, cells), 1).astype(f32) == column).astype(f32)
        one_hot[at, :] = hot.astype(bf16)

    copies[2].wait()

    spread = (iota((LANE, LANE), 0) // SUB == iota((LANE, LANE), 1) // SUB).astype(bf16)
    section_col = jnp.concatenate(section_cols, axis=0)
    in_section = (iota((bins, LANE), 1) % SUB).astype(f32) == section_col
    hot_bins = one_hot[:bins, :]
    for comp in range(3):
        for a in range(4):
            i = comp * 4 + a
            values = fluid[comp, a].reshape(16 * SUB, cells)
            for part, source in enumerate(split(values)):
                picked = jnp.where(in_section, dot_t(hot_bins, source), 0.0).astype(bf16)
                wide = dot(picked, spread)
                for g in range(groups):
                    block = wide[g * SUB : (g + 1) * SUB, :] * same
                    nodal[g, part * 96 + i * SUB : part * 96 + (i + 1) * SUB, :] = block.astype(bf16)

    for copy in copies[3:]:
        copy.wait()
    rates[...] = relax[...] * occupied[...]
    totals[...] = jnp.zeros(totals.shape, f32)

    def substep(first, turn, carry):
        for slot in range(GROUPS_TOGETHER):
            g = first + slot
            at = pl.ds(g * SUB, SUB)
            x = [parts_out[k, at, :] for k in range(3)]
            v = [parts_out[3 + k, at, :] for k in range(3)]
            rate = rates[at, :]
            step = strides[at, :]
            occ = occupied[at, :]
            la, lb, lc = [basis_values(x[k]) for k in range(3)]
            across = [lb[b] * lc[c] for b in range(4) for c in range(4)]
            high, low = split(jnp.concatenate(across, axis=0))
            by_high = dot(nodal[g], high)
            at_a = by_high[:96] + (by_high[96:] + dot(nodal[g, :96], low))
            pushes = []
            for k in range(3):
                rows = [at_a[(k * 4 + a) * SUB : (k * 4 + a + 1) * SUB, :] for a in range(4)]
                u = (la[0] * rows[0] + la[1] * rows[1]) + (la[2] * rows[2] + la[3] * rows[3])
                dv = rate * (u - v[k])
                moved = v[k] + dv
                parts_out[3 + k, at, :] = moved
                parts_out[k, at, :] = jnp.clip(x[k] + step * moved, -1.0, 1.0)
                pushes += [la[a] * dv for a in range(4)]
            weighs = [la[a] * la[a] * occ for a in range(4)]
            for n in range(16):
                for i in range(12):
                    j = i * 16 + n
                    sums[slot, j] = sums[slot, j] + across[n] * pushes[i]
            for n in range(16):
                square = across[n] * across[n]
                for a in range(4):
                    j = (12 + a) * 16 + n
                    sums[slot, j] = sums[slot, j] + square * weighs[a]
        return carry

    def over_lanes(slot, start):
        terms = [sums[slot, start + n] for n in range(LANE)]
        width = 1
        while width < LANE:
            upper = (lane8 // width) % 2 == 1
            terms = [
                jnp.where(upper, odd, even) + pltpu.roll(jnp.where(upper, even, odd), width, 1)
                for even, odd in zip(terms[0::2], terms[1::2])
            ]
            width *= 2
        return terms[0]

    for first in range(0, groups, GROUPS_TOGETHER):
        sums[...] = jnp.zeros(sums.shape, f32)
        lax.fori_loop(0, SUBSTEPS, functools.partial(substep, first), 0)
        for slot in range(GROUPS_TOGETHER):
            at = pl.ds((first + slot) * SUB, SUB)
            totals[at, :LANE] = over_lanes(slot, 0)
            totals[at, LANE:] = over_lanes(slot, LANE)

    in_section_rows = (iota((LANE, lanes_bins), 0) % SUB).astype(f32) == section_lanes
    hot_all = one_hot[...]
    spread_rows = (iota((LANE, 16), 0) // SUB == iota((LANE, 16), 1)).astype(bf16)
    by_node = jnp.concatenate([totals[:, :LANE].T, totals[:, LANE:].T], axis=0)

    for a in range(4):
        highs = []
        lows = []
        for i in (12 + a, a, 4 + a, 8 + a):
            high, low = split(by_node[i * 16 : (i + 1) * 16, :])
            wide = dot(spread_rows, high) + dot(spread_rows, low)
            high, low = split(jnp.where(in_section_rows, wide, 0.0))
            highs.append(high)
            lows.append(low)
        placed = dot(jnp.concatenate(highs + lows, axis=0), hot_all)
        placed = (placed[: 4 * LANE] + placed[4 * LANE :]).reshape(4, 4, 4, SUB, cells)
        scale = 1.0 / (mass[...][None, None] + placed[0])
        for comp in range(3):
            q_out[comp, a] = fluid[comp, a] - placed[1 + comp] * scale

    pack_columns(q_out, visc, speed, air_first, air_second)


def swap(values, axis, offset):
    count = lax.axis_size(axis)
    pairs = []
    for i in range(offset, count - 1, 2):
        pairs += [(i, i + 1), (i + 1, i)]
    return lax.ppermute(values, axis, pairs)


def local(
    fluid_velocity,
    viscosity,
    axial_speed,
    fluid_mass,
    positions,
    velocities,
    relax_rates,
    bin_element,
    bin_fill,
):
    sec_cells, air_cells = fluid_velocity.shape[2:]
    bins = positions.shape[0]
    groups = bins // SUB
    lanes_bins = -(-bins // LANE) * LANE
    field_shape = (3, 4, 4, 4, sec_cells, air_cells)
    field = jax.ShapeDtypeStruct(field_shape, f32)
    air_shape = jax.ShapeDtypeStruct((9, SUB, LANE), f32)
    strip_shape = jax.ShapeDtypeStruct((4, 4, 4, SUB, LANE), f32)
    tile_shape = jax.ShapeDtypeStruct((SUB, LANE), f32)
    face_shape = jax.ShapeDtypeStruct((FACE_BLOCKS, SUB, air_cells), f32)
    sent_shape = jax.ShapeDtypeStruct((COEFFICIENTS + 1, SUB, air_cells), f32)
    vmem = pl.BlockSpec(memory_space=pltpu.VMEM)
    hbm = pl.BlockSpec(memory_space=pltpu.HBM)
    params = pltpu.CompilerParams(vmem_limit_bytes=48 * 1024 * 1024)
    q, particles_out, air_first, air_second = pl.pallas_call(
        particle_kernel,
        out_shape=(field, jax.ShapeDtypeStruct((6, bins, LANE), f32), air_shape, air_shape),
        in_specs=[hbm] * 9,
        out_specs=(vmem,) * 4,
        scratch_shapes=[
            pltpu.VMEM((bins, LANE), f32),
            pltpu.VMEM((bins, LANE), f32),
            pltpu.VMEM((bins, LANE), f32),
            pltpu.VMEM((groups, 192, LANE), bf16),
            pltpu.VMEM((GROUPS_TOGETHER, 256, SUB, LANE), f32),
            pltpu.VMEM((lanes_bins, 256), f32),
            pltpu.VMEM((lanes_bins, air_cells), bf16),
            pltpu.VMEM((SUB, lanes_bins), f32),
            pltpu.VMEM(field_shape, f32),
            pltpu.VMEM(fluid_mass.shape, f32),
            pltpu.VMEM(relax_rates.shape, f32),
            pltpu.VMEM((1, bins), jnp.int32),
            pltpu.VMEM((1, bins), jnp.int32),
            pltpu.VMEM(viscosity.shape, f32),
            pltpu.VMEM(axial_speed.shape, f32),
            pltpu.SemaphoreType.DMA((9,)),
        ],
        compiler_params=params,
        name="particles",
    )(
        *(
            pltpu.with_memory_space_constraint(array, pltpu.HBM)
            for array in (
                fluid_velocity.reshape(field_shape),
                fluid_mass,
                positions.transpose(1, 0, 2),
                velocities.transpose(1, 0, 2),
                relax_rates,
                bin_element.reshape(1, bins),
                bin_fill.reshape(1, bins),
                viscosity,
                axial_speed,
            )
        )
    )

    def call(kernel, name, outputs, scratch, *operands):
        return pl.pallas_call(
            kernel,
            out_shape=outputs,
            in_specs=[vmem] * len(operands),
            out_specs=jax.tree.map(lambda _: vmem, outputs),
            scratch_shapes=[pltpu.VMEM(shape.shape, f32) for shape in scratch],
            compiler_params=params,
            cost_estimate=pl.CostEstimate(
                flops=30 * fluid_velocity.size, bytes_accessed=8 * fluid_velocity.size, transcendentals=0
            ),
            name=name,
        )(*operands)

    got_air = (swap(air_first, "airway", 0), swap(air_second, "airway", 1))
    w, *faces = call(
        main_kernel, "main", (field, face_shape, face_shape), (field,), q, viscosity, axial_speed
    )
    strip, strip_v, strip_g, *sent = call(
        strip_kernel,
        "strip",
        (strip_shape, tile_shape, tile_shape, sent_shape, sent_shape),
        (strip_shape,),
        q,
        viscosity,
        axial_speed,
        *got_air,
        *faces,
    )
    got = (swap(sent[0], "section", 0), swap(sent[1], "section", 1))
    w, strip = call(
        fourth_kernel,
        "fourth",
        (field, strip_shape),
        (),
        w,
        strip,
        viscosity,
        axial_speed,
        strip_v,
        strip_g,
    )
    mass_tile = jax.ShapeDtypeStruct(fluid_mass.shape, f32)
    q = call(
        edge_kernel,
        "edge",
        field,
        (field, field, strip_shape, strip_shape, mass_tile, mass_tile),
        w,
        strip,
        viscosity,
        axial_speed,
        strip_v,
        strip_g,
        *sent,
        *got,
    )
    return (q.reshape(3, NODES, sec_cells, air_cells), particles_out.transpose(1, 0, 2))


def solution(mesh):
    return jax.shard_map(
        local,
        mesh=mesh,
        in_specs=(
            P(None, None, "section", "airway"),
            P("section", "airway"),
            P("section", "airway"),
            P("section", "airway"),
            P(("airway", "section"), None, None),
            P(("airway", "section"), None, None),
            P(("airway", "section"), None),
            P(("airway", "section")),
            P(("airway", "section")),
        ),
        out_specs=(P(None, None, "section", "airway"), P(("airway", "section"), None, None)),
        check_vma=False,
    )
```

```python
import functools

import jax
import jax.numpy as jnp
import numpy as np
from jax import lax
from jax.experimental import pallas as pl
from jax.experimental.pallas import tpu as pltpu
from jax.sharding import PartitionSpec as P

NODES = 64
SUBSTEPS = 16
PASSES = 4
SUB = 8
LANE = 128
GROUPS_TOGETHER = 6

penalty_weight = 0.25
stride_step = 0.05
f32 = jnp.float32
bf16 = jnp.bfloat16


def iota(shape, dim):
    return lax.broadcasted_iota(jnp.int32, shape, dim)


def split(value):
    high = value.astype(bf16)
    low = (value - high.astype(f32)).astype(bf16)
    return high, low


def dot(a, b):
    return lax.dot_general(a, b, (((1,), (0,)), ((), ())), preferred_element_type=f32)


def dot_t(a, b):
    return lax.dot_general(a, b, (((1,), (1,)), ((), ())), preferred_element_type=f32)


def basis_values(x):
    square = x * x
    outer = 0.5625 * square - 0.0625
    inner = 1.6875 - 1.6875 * square
    outer_x = outer * x
    inner_x = inner * x
    third = inner * (1.0 / 3.0)
    return [outer - outer_x, third - inner_x, third + inner_x, outer + outer_x]


def is_even(axis):
    return lax.axis_index(axis) % 2 == 0


def pack_columns(q, visc, speed, first, second):
    cells = q.shape[-1]
    lane = iota((SUB, LANE), 1)
    even = is_even("airway")
    for tile in range(9):
        nxt = jnp.zeros((SUB, LANE), f32)
        prv = jnp.zeros((SUB, LANE), f32)
        for n in range(tile * 8, min(tile * 8 + 8, 66)):
            for comp in range(3):
                if n < NODES:
                    tail = q[comp, n // 16, n // 4 % 4, n % 4, :, cells - LANE :]
                    head = q[comp, n // 16, n // 4 % 4, n % 4, :, :LANE]
                else:
                    source = visc if n == NODES else speed
                    tail = source[:, cells - LANE :]
                    head = source[:, :LANE]
                start = 64 * (n // 4 % 2) + 16 * comp + 4 * (n % 4)
                here = (lane >= start) & (lane < start + 4)
                nxt = jnp.where(here, pltpu.roll(tail, (start + 4) % LANE, 1), nxt)
                prv = jnp.where(here, pltpu.roll(head, start, 1), prv)
        first[tile] = jnp.where(even, nxt, prv)
        second[tile] = jnp.where(even, prv, nxt)


def second_line(q, v_even, v_odd):
    even = v_even * ((q[0] + q[3]) - (q[1] + q[2]))
    odd = v_odd * ((q[3] - q[0]) - 3.0 * (q[2] - q[1]))
    third = odd * (1.0 / 3.0)
    return [even - odd, even - third, even + third, even + odd]


def advance_tile(
    load, store, v, g, beyond_next, beyond_prev, row_after, row_before, valid=None, drive=None
):
    lane = iota((SUB, LANE), 1)
    v_even, v_odd = v * 1.125, v * 3.375
    s_even, s_half = g * 1.125, g * 0.5
    for b in range(4):
        plane = [[load(a, b, c) for c in range(4)] for a in range(4)]
        along_c = [second_line(plane[a], v_even, v_odd) for a in range(4)]
        for c in range(4):
            line = [plane[a][c] for a in range(4)]
            rise = line[3] - line[0]
            even = (line[0] + line[3]) - (line[1] + line[2])
            odd = rise - 3.0 * (line[2] - line[1])
            l_even = v_even * even
            l_odd = v_odd * odd
            l_third = l_odd * (1.0 / 3.0)
            g_even = s_even * even
            g_odd = s_even * odd
            g_rise = s_half * rise
            g_even3 = g_even * (1.0 / 3.0)
            g_outer = g_rise + g_odd
            g_inner = g_rise - g_odd * (1.0 / 3.0)
            new = [
                (l_even + g_even) - (l_odd + g_outer),
                (l_even + g_even3) - (l_third + g_inner),
                (l_even - g_even3) + (l_third - g_inner),
                (l_even - g_even) + (l_odd - g_outer),
            ]
            new = [line[a] + (new[a] + along_c[a][c]) for a in range(4)]
            after = pltpu.roll(line[0], LANE - 1, 1)
            if beyond_next is not None:
                after = jnp.where(lane == LANE - 1, pltpu.roll(beyond_next(0, b, c), LANE - 1, 1), after)
            before = pltpu.roll(line[3], 1, 1)
            if beyond_prev is not None:
                before = jnp.where(lane == 0, pltpu.roll(beyond_prev(3, b, c), 1, 1), before)
            new[3] = new[3] + penalty_weight * (after - line[3])
            new[0] = new[0] + penalty_weight * (before - line[0])
            for a in range(4):
                store(a, b, c, new[a])
    return v_even, v_odd


def advance_rows(
    load, partial, store, v, row_after, row_before, valid=None, drive=None
):
    v_even, v_odd = v * 1.125, v * 3.375
    for a in range(4):
        for c in range(4):
            line = [load(a, b, c) for b in range(4)]
            new = second_line(line, v_even, v_odd)
            after = jnp.where(row_after, pltpu.roll(line[0], SUB - 1, 0), 0.0)
            before = jnp.where(row_before, pltpu.roll(line[3], 1, 0), 0.0)
            if drive is not None:
                more_after, more_before = drive(a * 4 + c)
                after = after + more_after
                before = before + more_before
            new[3] = new[3] + penalty_weight * (after - line[3])
            new[0] = new[0] + penalty_weight * (before - line[0])
            for b in range(4):
                value = partial(a, b, c) + new[b]
                store(a, b, c, value if valid is None else value * valid)


def advance_main(source, target, visc, speed, row_after, row_before, drive=None):
    tiles = source.shape[-1] // LANE

    def component(comp, carry):
        for j in range(tiles):
            at = pl.ds(j * LANE, LANE)
            at_next = pl.ds((j + 1) % tiles * LANE, LANE)
            at_prev = pl.ds((j - 1) % tiles * LANE, LANE)

            def load(a, b, c):
                return source[comp, a, b, c, :, at]

            def store(a, b, c, value):
                target[comp, a, b, c, :, at] = value

            v = visc[:, at]
            advance_tile(
                load,
                store,
                v,
                speed[:, at],
                lambda a, b, c: source[comp, a, b, c, :, at_next],
                lambda a, b, c: source[comp, a, b, c, :, at_prev],
                row_after,
                row_before,
            )
            advance_rows(
                load,
                lambda a, b, c: target[comp, a, b, c, :, at],
                store,
                v,
                row_after,
                row_before,
                drive=None if drive is None else functools.partial(drive, comp, at),
            )
        return carry

    lax.fori_loop(0, 3, component, 0)


def advance_strip(source, target, v, g, valid, row_after, row_before, drive=None):
    def load(a, b, c):
        return source[a, b, c]

    def store(a, b, c, value):
        target[a, b, c] = value

    advance_tile(load, store, v, g, None, None, row_after, row_before)
    advance_rows(
        load,
        lambda a, b, c: target[a, b, c],
        store,
        v,
        row_after,
        row_before,
        valid=valid,
        drive=drive,
    )


FACE_BLOCKS = PASSES * 3 * 2
STRIP_BLOCKS = PASSES
COEFFICIENTS = FACE_BLOCKS + STRIP_BLOCKS


def face_row(faces, turn, comp, i, at):
    return faces[(turn * 3 + comp) * 2 + i // SUB, i % SUB : i % SUB + 1, at]


def strip_at(turn, i):
    block = FACE_BLOCKS + turn // 2 * 2 + i // SUB
    return block, i % SUB, pl.ds(turn % 2 * LANE, LANE)


def block_rows():
    row = iota((SUB, LANE), 0)
    return row != SUB - 1, row != 0


def strip_valid():
    lane = iota((SUB, LANE), 1)
    place = lane % 16
    index = lax.axis_index("airway")
    first = (index == 0).astype(f32)
    last = (index == lax.axis_size("airway") - 1).astype(f32)
    left = ((lane < 64) & (place < 4)).astype(f32)
    right = ((lane >= 64) & (place >= 8)).astype(f32)
    return 1.0 - left * first - right * last


def main_kernel(q, visc, speed, out, faces_first, faces_second, spare):
    row_after, row_before = block_rows()
    even = is_even("section")

    def pack(source, turn):
        for comp in range(3):
            for i in range(16):
                tail = source[comp, i // 4, 3, i % 4, SUB - 1 : SUB, :]
                head = source[comp, i // 4, 0, i % 4, 0:1, :]
                block = (turn * 3 + comp) * 2 + i // SUB
                at = pl.ds(i % SUB, 1)
                faces_first[block, at, :] = jnp.where(even, tail, head)
                faces_second[block, at, :] = jnp.where(even, head, tail)

    pack(q, 0)
    advance_main(q, out, visc, speed, row_after, row_before)
    pack(out, 1)
    advance_main(out, spare, visc, speed, row_after, row_before)
    pack(spare, 2)
    advance_main(spare, out, visc, speed, row_after, row_before)
    pack(out, 3)


def strip_kernel(
    q,
    visc,
    speed,
    air_first,
    air_second,
    faces_first,
    faces_second,
    out,
    strip_v,
    strip_g,
    sent_first,
    sent_second,
    spare,
):
    cells = q.shape[-1]
    lane = iota((SUB, LANE), 1)
    place = lane % 16
    forward = is_even("airway")
    left = (lane < 64) & (place < 4)
    right = (lane >= 64) & (place >= 8)

    def assemble(n, heads, tails):
        total = jnp.zeros((SUB, LANE), f32)
        for comp in range(3):
            base = 16 * comp
            total = jnp.where(lane // 16 == comp, pltpu.roll(heads[comp], base + 4, 1), total)
            total = jnp.where(
                lane // 16 == comp + 4, pltpu.roll(tails[comp], (base + 72) % LANE, 1), total
            )
        one = air_first[n // 8]
        two = air_second[n // 8]
        offset = 64 * (n // 4 % 2) + 4 * (n % 4)
        from_next = jnp.where(forward, one, two)
        from_prev = jnp.where(forward, two, one)
        total = jnp.where(left, pltpu.roll(from_prev, (LANE - offset) % LANE, 1), total)
        total = jnp.where(right, pltpu.roll(from_next, (LANE + 72 - offset) % LANE, 1), total)
        return jnp.where(place < 12, total, 0.0)

    for n in range(NODES):
        a, b, c = n // 16, n // 4 % 4, n % 4
        out[a, b, c] = assemble(
            n,
            [q[k, a, b, c, :, :LANE] for k in range(3)],
            [q[k, a, b, c, :, cells - LANE :] for k in range(3)],
        )
    strip_v[...] = assemble(NODES, [visc[:, :LANE]] * 3, [visc[:, cells - LANE :]] * 3)
    strip_g[...] = assemble(NODES + 1, [speed[:, :LANE]] * 3, [speed[:, cells - LANE :]] * 3)

    row_after, row_before = block_rows()
    even = is_even("section")
    sent_first[:FACE_BLOCKS] = faces_first[...]
    sent_second[:FACE_BLOCKS] = faces_second[...]

    def send(block, row, at, tail, head):
        sent_first[block, row : row + 1, at] = jnp.where(even, tail, head)
        sent_second[block, row : row + 1, at] = jnp.where(even, head, tail)

    def pack(source, turn):
        for i in range(16):
            block, row, at = strip_at(turn, i)
            send(
                block,
                row,
                at,
                source[i // 4, 3, i % 4, SUB - 1 : SUB, :],
                source[i // 4, 0, i % 4, 0:1, :],
            )

    everything = pl.ds(0, cells)
    sent_first[COEFFICIENTS] = jnp.zeros((SUB, cells), f32)
    sent_second[COEFFICIENTS] = jnp.zeros((SUB, cells), f32)
    send(COEFFICIENTS, 0, everything, visc[SUB - 1 : SUB, :], visc[0:1, :])
    send(COEFFICIENTS, 1, everything, speed[SUB - 1 : SUB, :], speed[0:1, :])
    send(COEFFICIENTS, 2, pl.ds(0, LANE), strip_v[SUB - 1 : SUB, :], strip_v[0:1, :])
    send(COEFFICIENTS, 2, pl.ds(LANE, LANE), strip_g[SUB - 1 : SUB, :], strip_g[0:1, :])

    v, g, valid = strip_v[...], strip_g[...], strip_valid()
    pack(out, 0)
    advance_strip(out, spare, v, g, valid, row_after, row_before)
    pack(spare, 1)
    advance_strip(spare, out, v, g, valid, row_after, row_before)
    pack(out, 2)
    advance_strip(out, spare, v, g, valid, row_after, row_before)
    pack(spare, 3)
    out[...] = spare[...]


def fourth_kernel(w, strip, visc, speed, strip_v, strip_g, w_out, strip_out):
    row_after, row_before = block_rows()
    advance_main(w, w_out, visc, speed, row_after, row_before)
    advance_strip(
        strip, strip_out, strip_v[...], strip_g[...], strip_valid(), row_after, row_before
    )


def edge_kernel(
    w,
    strip,
    visc,
    speed,
    strip_v,
    strip_g,
    sent_first,
    sent_second,
    got_first,
    got_second,
    out,
    e_one,
    e_two,
    z_one,
    z_two,
    e_visc,
    e_speed,
):
    cells = w.shape[-1]
    tiles = cells // LANE
    row = iota((SUB, LANE), 0)
    lane = iota((SUB, LANE), 1)
    even = is_even("section")
    index = lax.axis_index("section")
    has_prev = index > 0
    has_next = index < lax.axis_size("section") - 1
    row_after = (row != SUB - 1) & ((row != 0) | has_prev)
    row_before = (row != 0) & ((row != SUB - 1) | has_next)

    def rows_of(own, prev_row, next_row):
        moved = jnp.where(row == 1, pltpu.roll(own, 1, 0), 0.0)
        moved = jnp.where(row == 2, pltpu.roll(own, 1, 0), moved)
        moved = jnp.where((row == 5) | (row == 6), pltpu.roll(own, SUB - 1, 0), moved)
        moved = jnp.where(row == 0, jnp.broadcast_to(prev_row, (SUB, LANE)), moved)
        return jnp.where(row == SUB - 1, jnp.broadcast_to(next_row, (SUB, LANE)), moved)

    def received(block, r, at):
        one = got_first[block, r : r + 1, at]
        two = got_second[block, r : r + 1, at]
        return jnp.where(even, two, one), jnp.where(even, one, two)

    for j in range(tiles):
        at = pl.ds(j * LANE, LANE)
        e_visc[:, at] = rows_of(visc[:, at], *received(COEFFICIENTS, 0, at))
        e_speed[:, at] = rows_of(speed[:, at], *received(COEFFICIENTS, 1, at))
    z_v = rows_of(strip_v[...], *received(COEFFICIENTS, 2, pl.ds(0, LANE)))
    z_g = rows_of(strip_g[...], *received(COEFFICIENTS, 2, pl.ds(LANE, LANE)))
    valid = strip_valid()

    def forcing(pick):
        one = jnp.broadcast_to(pick(got_first), (SUB, LANE))
        two = jnp.broadcast_to(pick(got_second), (SUB, LANE))
        own_one = jnp.broadcast_to(pick(sent_first), (SUB, LANE))
        own_two = jnp.broadcast_to(pick(sent_second), (SUB, LANE))
        from_next = jnp.where(even, one, two)
        from_prev = jnp.where(even, two, one)
        own_next = jnp.where(even, own_one, own_two)
        own_prev = jnp.where(even, own_two, own_one)
        after = jnp.where(
            row == 6, from_next, jnp.where((row == 0) & has_prev, own_prev, 0.0)
        )
        before = jnp.where(
            row == 1, from_prev, jnp.where((row == SUB - 1) & has_next, own_next, 0.0)
        )
        return after, before

    def drive(turn, comp, at, i):
        return forcing(lambda faces: face_row(faces, turn, comp, i, at))

    def drive_strip(turn, i):
        block, r, at = strip_at(turn, i)
        return forcing(lambda faces: faces[block, r : r + 1, at])

    def first_component(comp, carry):
        for j in range(tiles):
            at = pl.ds(j * LANE, LANE)
            for i in range(16):
                a, c = i // 4, i % 4
                after, before = drive(0, comp, at, i)
                e_one[comp, a, 3, c, :, at] = penalty_weight * after
                e_one[comp, a, 0, c, :, at] = penalty_weight * before
                for b in (1, 2):
                    e_one[comp, a, b, c, :, at] = jnp.zeros((SUB, LANE), f32)
        return carry

    lax.fori_loop(0, 3, first_component, 0)
    for i in range(16):
        a, c = i // 4, i % 4
        after, before = drive_strip(0, i)
        z_one[a, 3, c] = penalty_weight * after * valid
        z_one[a, 0, c] = penalty_weight * before * valid
        for b in (1, 2):
            z_one[a, b, c] = jnp.zeros((SUB, LANE), f32)

    for turn, (source, target, z_source, z_target) in enumerate(
        ((e_one, e_two, z_one, z_two), (e_two, e_one, z_two, z_one), (e_one, e_two, z_one, z_two)),
        1,
    ):
        advance_main(
            source,
            target,
            e_visc,
            e_speed,
            row_after,
            row_before,
            functools.partial(drive, turn),
        )
        advance_strip(
            z_source,
            z_target,
            z_v,
            z_g,
            valid,
            row_after,
            row_before,
            functools.partial(drive_strip, turn),
        )

    low = row < 2
    high = row >= 6

    def back(effect):
        return jnp.where(
            low, pltpu.roll(effect, SUB - 1, 0), jnp.where(high, pltpu.roll(effect, 1, 0), 0.0)
        )

    for n in range(NODES):
        a, b, c = n // 16, n // 4 % 4, n % 4
        z_one[a, b, c] = strip[a, b, c] + back(z_two[a, b, c])

    def finish(comp, carry):
        for n in range(NODES):
            a, b, c = n // 16, n // 4 % 4, n % 4
            edge = z_one[a, b, c]
            for j in range(tiles):
                at = pl.ds(j * LANE, LANE)
                value = w[comp, a, b, c, :, at] + back(e_two[comp, a, b, c, :, at])
                if j == 0:
                    value = jnp.where(lane < 4, pltpu.roll(edge, LANE - 4 - 16 * comp, 1), value)
                if j == tiles - 1:
                    value = jnp.where(
                        lane >= LANE - 4, pltpu.roll(edge, LANE - 4 - 68 - 16 * comp, 1), value
                    )
                out[comp, a, b, c, :, at] = value
        return carry

    lax.fori_loop(0, 3, finish, 0)


def particle_kernel(
    fluid_hbm,
    mass_hbm,
    positions,
    velocities,
    relax_hbm,
    element_hbm,
    fill_hbm,
    visc_hbm,
    speed_hbm,
    q_out,
    parts_out,
    air_first,
    air_second,
    rates,
    strides,
    occupied,
    nodal,
    sums_even,
    sums_odd,
    totals,
    one_hot,
    rows_ref,
    fluid,
    mass,
    relax,
    element_row,
    fill_row,
    visc,
    speed,
    arrived,
):
    copies = [
        pltpu.make_async_copy(source, target, arrived.at[i])
        for i, (source, target) in enumerate(
            (
                (element_hbm, element_row),
                (fill_hbm, fill_row),
                (fluid_hbm, fluid),
                (relax_hbm, relax),
                (positions, parts_out.at[0:3]),
                (velocities, parts_out.at[3:6]),
                (mass_hbm, mass),
                (visc_hbm, visc),
                (speed_hbm, speed),
            )
        )
    ]
    for copy in copies:
        copy.start()
    bins = positions.shape[1]
    groups = bins // SUB
    lanes_bins = one_hot.shape[0]
    cells = fluid.shape[-1]
    row8 = iota((SUB, LANE), 0)
    lane8 = iota((SUB, LANE), 1)
    same = (lane8 % SUB == row8).astype(f32)

    copies[0].wait()
    copies[1].wait()

    rows_ref[...] = jnp.full(rows_ref.shape, -1.0, f32)
    rows_ref[0:1, :bins] = element_row[...].astype(f32)
    rows_ref[1:2, :bins] = fill_row[...].astype(f32)
    element_lanes = rows_ref[0:1, :]
    section_lanes = jnp.zeros_like(element_lanes)
    for s in range(1, SUB):
        section_lanes = section_lanes + (element_lanes >= float(s * cells)).astype(f32)

    lane_bins = iota((SUB, lanes_bins), 1)
    row_bins = iota((SUB, lanes_bins), 0)
    one_hot[...] = jnp.zeros(one_hot.shape, bf16)
    for g in range(groups):
        own = lane_bins == row_bins + g * SUB
        element = jnp.sum(jnp.where(own, element_lanes, 0.0), axis=1, keepdims=True)
        fill = jnp.sum(jnp.where(own, rows_ref[1:2, :], 0.0), axis=1, keepdims=True)
        section = jnp.zeros_like(element)
        for s in range(1, SUB):
            section = section + (element >= float(s * cells)).astype(f32)
        column = element - section * float(cells)
        at = pl.ds(g * SUB, SUB)
        occ = (lane8.astype(f32) < fill).astype(f32)
        occupied[at, :] = occ
        strides[at, :] = occ * stride_step
        hot = (iota((SUB, cells), 1).astype(f32) == column).astype(f32)
        one_hot[at, :] = hot.astype(bf16)

    copies[2].wait()

    spread = (iota((LANE, LANE), 0) // SUB == iota((LANE, LANE), 1) // SUB).astype(bf16)
    in_section_rows = (iota((LANE, lanes_bins), 0) % SUB).astype(f32) == section_lanes
    hot_all = one_hot[...]
    sources = []
    for comp in range(3):
        for a in range(4):
            sources += split(fluid[comp, a].reshape(16 * SUB, cells))
    found = dot_t(jnp.concatenate(sources, axis=0), hot_all)
    picked = [
        jnp.where(in_section_rows, found[k * LANE : (k + 1) * LANE], 0.0).T.astype(bf16)
        for k in range(24)
    ]
    wide = dot(jnp.concatenate(picked, axis=0), spread)
    for i in range(12):
        for part in range(2):
            rows = wide[(i * 2 + part) * lanes_bins : (i * 2 + part + 1) * lanes_bins]
            for g in range(groups):
                block = rows[g * SUB : (g + 1) * SUB, :] * same
                start = part * 96 + i * SUB
                nodal[g, start : start + SUB, :] = block.astype(bf16)

    for copy in copies[3:]:
        copy.wait()
    rates[...] = relax[...] * occupied[...]
    totals[...] = jnp.zeros(totals.shape, f32)

    sums = (sums_even, sums_odd)

    def sum_lanes(first, turn):
        buffer = sums[first // GROUPS_TOGETHER % 2]
        for slot in range(GROUPS_TOGETHER):
            at = pl.ds((first + slot) * SUB, SUB)
            total = totals[turn // 8, at, :]
            for n in range(16):
                j = turn * 16 + n
                over_lanes = jnp.sum(buffer[slot, j], axis=1, keepdims=True)
                total = jnp.where(lane8 == j % LANE, over_lanes, total)
                buffer[slot, j] = jnp.zeros((SUB, LANE), f32)
            totals[turn // 8, at, :] = total

    def substep(first, turn, carry):
        if first:
            sum_lanes(first - GROUPS_TOGETHER, turn)
        buffer = sums[first // GROUPS_TOGETHER % 2]
        for slot in range(GROUPS_TOGETHER):
            g = first + slot
            at = pl.ds(g * SUB, SUB)
            x = [parts_out[k, at, :] for k in range(3)]
            v = [parts_out[3 + k, at, :] for k in range(3)]
            rate = rates[at, :]
            step = strides[at, :]
            occ = occupied[at, :]
            la, lb, lc = [basis_values(x[k]) for k in range(3)]
            across = [lb[b] * lc[c] for b in range(4) for c in range(4)]
            high, low = split(jnp.concatenate(across, axis=0))
            by_high = dot(nodal[g], high)
            at_a = by_high[:96] + (by_high[96:] + dot(nodal[g, :96], low))
            pushes = []
            for k in range(3):
                rows = [at_a[(k * 4 + a) * SUB : (k * 4 + a + 1) * SUB, :] for a in range(4)]
                u = (la[0] * rows[0] + la[1] * rows[1]) + (la[2] * rows[2] + la[3] * rows[3])
                dv = rate * (u - v[k])
                moved = v[k] + dv
                parts_out[3 + k, at, :] = moved
                parts_out[k, at, :] = jnp.clip(x[k] + step * moved, -1.0, 1.0)
                pushes += [la[a] * dv for a in range(4)]
            weighs = [la[a] * la[a] * occ for a in range(4)]
            for n in range(16):
                for i in range(12):
                    j = i * 16 + n
                    buffer[slot, j] = buffer[slot, j] + across[n] * pushes[i]
            for n in range(16):
                square = across[n] * across[n]
                for a in range(4):
                    j = (12 + a) * 16 + n
                    buffer[slot, j] = buffer[slot, j] + square * weighs[a]
        return carry

    for buffer in sums:
        buffer[...] = jnp.zeros(buffer.shape, f32)
    for first in range(0, groups, GROUPS_TOGETHER):
        lax.fori_loop(0, SUBSTEPS, functools.partial(substep, first), 0)
    for turn in range(16):
        sum_lanes(groups - GROUPS_TOGETHER, turn)

    spread_rows = (iota((LANE, 16), 0) // SUB == iota((LANE, 16), 1)).astype(bf16)
    by_node = jnp.concatenate([totals[0].T, totals[1].T], axis=0)

    for a in range(4):
        highs = []
        lows = []
        for i in (12 + a, a, 4 + a, 8 + a):
            high, low = split(by_node[i * 16 : (i + 1) * 16, :])
            wide = dot(spread_rows, high) + dot(spread_rows, low)
            high, low = split(jnp.where(in_section_rows, wide, 0.0))
            highs.append(high)
            lows.append(low)
        placed = dot(jnp.concatenate(highs + lows, axis=0), hot_all)
        placed = (placed[: 4 * LANE] + placed[4 * LANE :]).reshape(4, 4, 4, SUB, cells)
        scale = 1.0 / (mass[...][None, None] + placed[0])
        for comp in range(3):
            q_out[comp, a] = fluid[comp, a] - placed[1 + comp] * scale

    pack_columns(q_out, visc, speed, air_first, air_second)


def swap(values, axis, offset):
    count = lax.axis_size(axis)
    pairs = []
    for i in range(offset, count - 1, 2):
        pairs += [(i, i + 1), (i + 1, i)]
    return lax.ppermute(values, axis, pairs)


def local(
    fluid_velocity,
    viscosity,
    axial_speed,
    fluid_mass,
    positions,
    velocities,
    relax_rates,
    bin_element,
    bin_fill,
):
    sec_cells, air_cells = fluid_velocity.shape[2:]
    bins = positions.shape[0]
    groups = bins // SUB
    lanes_bins = -(-bins // LANE) * LANE
    field_shape = (3, 4, 4, 4, sec_cells, air_cells)
    field = jax.ShapeDtypeStruct(field_shape, f32)
    air_shape = jax.ShapeDtypeStruct((9, SUB, LANE), f32)
    strip_shape = jax.ShapeDtypeStruct((4, 4, 4, SUB, LANE), f32)
    tile_shape = jax.ShapeDtypeStruct((SUB, LANE), f32)
    face_shape = jax.ShapeDtypeStruct((FACE_BLOCKS, SUB, air_cells), f32)
    sent_shape = jax.ShapeDtypeStruct((COEFFICIENTS + 1, SUB, air_cells), f32)
    vmem = pl.BlockSpec(memory_space=pltpu.VMEM)
    hbm = pl.BlockSpec(memory_space=pltpu.HBM)
    params = pltpu.CompilerParams(vmem_limit_bytes=48 * 1024 * 1024)
    q, particles_out, air_first, air_second = pl.pallas_call(
        particle_kernel,
        out_shape=(field, jax.ShapeDtypeStruct((6, bins, LANE), f32), air_shape, air_shape),
        in_specs=[hbm] * 9,
        out_specs=(vmem,) * 4,
        scratch_shapes=[
            pltpu.VMEM((bins, LANE), f32),
            pltpu.VMEM((bins, LANE), f32),
            pltpu.VMEM((bins, LANE), f32),
            pltpu.VMEM((groups, 192, LANE), bf16),
            pltpu.VMEM((GROUPS_TOGETHER, 256, SUB, LANE), f32),
            pltpu.VMEM((GROUPS_TOGETHER, 256, SUB, LANE), f32),
            pltpu.VMEM((2, lanes_bins, LANE), f32),
            pltpu.VMEM((lanes_bins, air_cells), bf16),
            pltpu.VMEM((SUB, lanes_bins), f32),
            pltpu.VMEM(field_shape, f32),
            pltpu.VMEM(fluid_mass.shape, f32),
            pltpu.VMEM(relax_rates.shape, f32),
            pltpu.VMEM((1, bins), jnp.int32),
            pltpu.VMEM((1, bins), jnp.int32),
            pltpu.VMEM(viscosity.shape, f32),
            pltpu.VMEM(axial_speed.shape, f32),
            pltpu.SemaphoreType.DMA((9,)),
        ],
        compiler_params=params,
        name="particles",
    )(
        *(
            pltpu.with_memory_space_constraint(array, pltpu.HBM)
            for array in (
                fluid_velocity.reshape(field_shape),
                fluid_mass,
                positions.transpose(1, 0, 2),
                velocities.transpose(1, 0, 2),
                relax_rates,
                bin_element.reshape(1, bins),
                bin_fill.reshape(1, bins),
                viscosity,
                axial_speed,
            )
        )
    )

    def call(kernel, name, outputs, scratch, *operands):
        return pl.pallas_call(
            kernel,
            out_shape=outputs,
            in_specs=[vmem] * len(operands),
            out_specs=jax.tree.map(lambda _: vmem, outputs),
            scratch_shapes=[pltpu.VMEM(shape.shape, f32) for shape in scratch],
            compiler_params=params,
            cost_estimate=pl.CostEstimate(
                flops=30 * fluid_velocity.size, bytes_accessed=8 * fluid_velocity.size, transcendentals=0
            ),
            name=name,
        )(*operands)

    got_air = (swap(air_first, "airway", 0), swap(air_second, "airway", 1))
    w, *faces = call(
        main_kernel, "main", (field, face_shape, face_shape), (field,), q, viscosity, axial_speed
    )
    strip, strip_v, strip_g, *sent = call(
        strip_kernel,
        "strip",
        (strip_shape, tile_shape, tile_shape, sent_shape, sent_shape),
        (strip_shape,),
        q,
        viscosity,
        axial_speed,
        *got_air,
        *faces,
    )
    got = (swap(sent[0], "section", 0), swap(sent[1], "section", 1))
    w, strip = call(
        fourth_kernel,
        "fourth",
        (field, strip_shape),
        (),
        w,
        strip,
        viscosity,
        axial_speed,
        strip_v,
        strip_g,
    )
    mass_tile = jax.ShapeDtypeStruct(fluid_mass.shape, f32)
    q = call(
        edge_kernel,
        "edge",
        field,
        (field, field, strip_shape, strip_shape, mass_tile, mass_tile),
        w,
        strip,
        viscosity,
        axial_speed,
        strip_v,
        strip_g,
        *sent,
        *got,
    )
    return (q.reshape(3, NODES, sec_cells, air_cells), particles_out.transpose(1, 0, 2))


def solution(mesh):
    return jax.shard_map(
        local,
        mesh=mesh,
        in_specs=(
            P(None, None, "section", "airway"),
            P("section", "airway"),
            P("section", "airway"),
            P("section", "airway"),
            P(("airway", "section"), None, None),
            P(("airway", "section"), None, None),
            P(("airway", "section"), None),
            P(("airway", "section")),
            P(("airway", "section")),
        ),
        out_specs=(P(None, None, "section", "airway"), P(("airway", "section"), None, None)),
        check_vma=False,
    )
```

```python
import functools

import jax
import jax.numpy as jnp
import numpy as np
from jax import lax
from jax.experimental import pallas as pl
from jax.experimental.pallas import tpu as pltpu
from jax.sharding import PartitionSpec as P

NODES = 64
SUBSTEPS = 16
PASSES = 4
SUB = 8
LANE = 128
GROUPS_TOGETHER = 6

penalty_weight = 0.25
stride_step = 0.05
f32 = jnp.float32
bf16 = jnp.bfloat16


def iota(shape, dim):
    return lax.broadcasted_iota(jnp.int32, shape, dim)


def split(value):
    high = value.astype(bf16)
    low = (value - high.astype(f32)).astype(bf16)
    return high, low


def dot(a, b):
    return lax.dot_general(a, b, (((1,), (0,)), ((), ())), preferred_element_type=f32)


def dot_t(a, b):
    return lax.dot_general(a, b, (((1,), (1,)), ((), ())), preferred_element_type=f32)


def basis_values(x):
    square = x * x
    outer = 0.5625 * square - 0.0625
    inner = 1.6875 - 1.6875 * square
    outer_x = outer * x
    inner_x = inner * x
    third = inner * (1.0 / 3.0)
    return [outer - outer_x, third - inner_x, third + inner_x, outer + outer_x]


def is_even(axis):
    return lax.axis_index(axis) % 2 == 0


def pack_columns(q, visc, speed, first, second):
    cells = q.shape[-1]
    lane = iota((SUB, LANE), 1)
    even = is_even("airway")
    for tile in range(9):
        nxt = jnp.zeros((SUB, LANE), f32)
        prv = jnp.zeros((SUB, LANE), f32)
        for n in range(tile * 8, min(tile * 8 + 8, 66)):
            for comp in range(3):
                if n < NODES:
                    tail = q[comp, n // 16, n // 4 % 4, n % 4, :, cells - LANE :]
                    head = q[comp, n // 16, n // 4 % 4, n % 4, :, :LANE]
                else:
                    source = visc if n == NODES else speed
                    tail = source[:, cells - LANE :]
                    head = source[:, :LANE]
                start = 64 * (n // 4 % 2) + 16 * comp + 4 * (n % 4)
                here = (lane >= start) & (lane < start + 4)
                nxt = jnp.where(here, pltpu.roll(tail, (start + 4) % LANE, 1), nxt)
                prv = jnp.where(here, pltpu.roll(head, start, 1), prv)
        first[tile] = jnp.where(even, nxt, prv)
        second[tile] = jnp.where(even, prv, nxt)


def second_line(q, v_even, v_odd):
    even = v_even * ((q[0] + q[3]) - (q[1] + q[2]))
    odd = v_odd * ((q[3] - q[0]) - 3.0 * (q[2] - q[1]))
    third = odd * (1.0 / 3.0)
    return [even - odd, even - third, even + third, even + odd]


def advance_tile(
    load, store, v, g, beyond_next, beyond_prev, row_after, row_before, valid=None, drive=None
):
    lane = iota((SUB, LANE), 1)
    v_even, v_odd = v * 1.125, v * 3.375
    s_even, s_half = g * 1.125, g * 0.5
    for b in range(4):
        plane = [[load(a, b, c) for c in range(4)] for a in range(4)]
        along_c = [second_line(plane[a], v_even, v_odd) for a in range(4)]
        for c in range(4):
            line = [plane[a][c] for a in range(4)]
            rise = line[3] - line[0]
            even = (line[0] + line[3]) - (line[1] + line[2])
            odd = rise - 3.0 * (line[2] - line[1])
            l_even = v_even * even
            l_odd = v_odd * odd
            l_third = l_odd * (1.0 / 3.0)
            g_even = s_even * even
            g_odd = s_even * odd
            g_rise = s_half * rise
            g_even3 = g_even * (1.0 / 3.0)
            g_outer = g_rise + g_odd
            g_inner = g_rise - g_odd * (1.0 / 3.0)
            new = [
                (l_even + g_even) - (l_odd + g_outer),
                (l_even + g_even3) - (l_third + g_inner),
                (l_even - g_even3) + (l_third - g_inner),
                (l_even - g_even) + (l_odd - g_outer),
            ]
            new = [line[a] + (new[a] + along_c[a][c]) for a in range(4)]
            after = pltpu.roll(line[0], LANE - 1, 1)
            if beyond_next is not None:
                after = jnp.where(lane == LANE - 1, pltpu.roll(beyond_next(0, b, c), LANE - 1, 1), after)
            before = pltpu.roll(line[3], 1, 1)
            if beyond_prev is not None:
                before = jnp.where(lane == 0, pltpu.roll(beyond_prev(3, b, c), 1, 1), before)
            new[3] = new[3] + penalty_weight * (after - line[3])
            new[0] = new[0] + penalty_weight * (before - line[0])
            for a in range(4):
                store(a, b, c, new[a])
    return v_even, v_odd


def advance_rows(
    load, partial, store, v, row_after, row_before, valid=None, drive=None
):
    v_even, v_odd = v * 1.125, v * 3.375
    for a in range(4):
        for c in range(4):
            line = [load(a, b, c) for b in range(4)]
            new = second_line(line, v_even, v_odd)
            after = jnp.where(row_after, pltpu.roll(line[0], SUB - 1, 0), 0.0)
            before = jnp.where(row_before, pltpu.roll(line[3], 1, 0), 0.0)
            if drive is not None:
                more_after, more_before = drive(a * 4 + c)
                after = after + more_after
                before = before + more_before
            new[3] = new[3] + penalty_weight * (after - line[3])
            new[0] = new[0] + penalty_weight * (before - line[0])
            for b in range(4):
                value = partial(a, b, c) + new[b]
                store(a, b, c, value if valid is None else value * valid)


def advance_main(source, target, visc, speed, row_after, row_before, drive=None):
    tiles = source.shape[-1] // LANE

    def component(comp, carry):
        for j in range(tiles):
            at = pl.ds(j * LANE, LANE)
            at_next = pl.ds((j + 1) % tiles * LANE, LANE)
            at_prev = pl.ds((j - 1) % tiles * LANE, LANE)

            def load(a, b, c):
                return source[comp, a, b, c, :, at]

            def store(a, b, c, value):
                target[comp, a, b, c, :, at] = value

            v = visc[:, at]
            advance_tile(
                load,
                store,
                v,
                speed[:, at],
                lambda a, b, c: source[comp, a, b, c, :, at_next],
                lambda a, b, c: source[comp, a, b, c, :, at_prev],
                row_after,
                row_before,
            )
            advance_rows(
                load,
                lambda a, b, c: target[comp, a, b, c, :, at],
                store,
                v,
                row_after,
                row_before,
                drive=None if drive is None else functools.partial(drive, comp, at),
            )
        return carry

    lax.fori_loop(0, 3, component, 0)


def advance_strip(source, target, v, g, valid, row_after, row_before, drive=None):
    def load(a, b, c):
        return source[a, b, c]

    def store(a, b, c, value):
        target[a, b, c] = value

    advance_tile(load, store, v, g, None, None, row_after, row_before)
    advance_rows(
        load,
        lambda a, b, c: target[a, b, c],
        store,
        v,
        row_after,
        row_before,
        valid=valid,
        drive=drive,
    )


FACE_BLOCKS = PASSES * 3 * 2
STRIP_BLOCKS = PASSES
COEFFICIENTS = FACE_BLOCKS + STRIP_BLOCKS


def face_row(faces, turn, comp, i, at):
    return faces[(turn * 3 + comp) * 2 + i // SUB, i % SUB : i % SUB + 1, at]


def strip_at(turn, i):
    block = FACE_BLOCKS + turn // 2 * 2 + i // SUB
    return block, i % SUB, pl.ds(turn % 2 * LANE, LANE)


def block_rows():
    row = iota((SUB, LANE), 0)
    return row != SUB - 1, row != 0


def strip_valid():
    lane = iota((SUB, LANE), 1)
    place = lane % 16
    index = lax.axis_index("airway")
    first = (index == 0).astype(f32)
    last = (index == lax.axis_size("airway") - 1).astype(f32)
    left = ((lane < 64) & (place < 4)).astype(f32)
    right = ((lane >= 64) & (place >= 8)).astype(f32)
    return 1.0 - left * first - right * last


def main_kernel(q, visc, speed, out, faces_first, faces_second, spare):
    row_after, row_before = block_rows()
    even = is_even("section")

    def pack(source, turn):
        for comp in range(3):
            for i in range(16):
                tail = source[comp, i // 4, 3, i % 4, SUB - 1 : SUB, :]
                head = source[comp, i // 4, 0, i % 4, 0:1, :]
                block = (turn * 3 + comp) * 2 + i // SUB
                at = pl.ds(i % SUB, 1)
                faces_first[block, at, :] = jnp.where(even, tail, head)
                faces_second[block, at, :] = jnp.where(even, head, tail)

    pack(q, 0)
    advance_main(q, out, visc, speed, row_after, row_before)
    pack(out, 1)
    advance_main(out, spare, visc, speed, row_after, row_before)
    pack(spare, 2)
    advance_main(spare, out, visc, speed, row_after, row_before)
    pack(out, 3)


def strip_kernel(
    q,
    visc,
    speed,
    air_first,
    air_second,
    faces_first,
    faces_second,
    out,
    strip_v,
    strip_g,
    sent_first,
    sent_second,
    spare,
):
    cells = q.shape[-1]
    lane = iota((SUB, LANE), 1)
    place = lane % 16
    forward = is_even("airway")
    left = (lane < 64) & (place < 4)
    right = (lane >= 64) & (place >= 8)

    def assemble(n, heads, tails):
        total = jnp.zeros((SUB, LANE), f32)
        for comp in range(3):
            base = 16 * comp
            total = jnp.where(lane // 16 == comp, pltpu.roll(heads[comp], base + 4, 1), total)
            total = jnp.where(
                lane // 16 == comp + 4, pltpu.roll(tails[comp], (base + 72) % LANE, 1), total
            )
        one = air_first[n // 8]
        two = air_second[n // 8]
        offset = 64 * (n // 4 % 2) + 4 * (n % 4)
        from_next = jnp.where(forward, one, two)
        from_prev = jnp.where(forward, two, one)
        total = jnp.where(left, pltpu.roll(from_prev, (LANE - offset) % LANE, 1), total)
        total = jnp.where(right, pltpu.roll(from_next, (LANE + 72 - offset) % LANE, 1), total)
        return jnp.where(place < 12, total, 0.0)

    for n in range(NODES):
        a, b, c = n // 16, n // 4 % 4, n % 4
        out[a, b, c] = assemble(
            n,
            [q[k, a, b, c, :, :LANE] for k in range(3)],
            [q[k, a, b, c, :, cells - LANE :] for k in range(3)],
        )
    strip_v[...] = assemble(NODES, [visc[:, :LANE]] * 3, [visc[:, cells - LANE :]] * 3)
    strip_g[...] = assemble(NODES + 1, [speed[:, :LANE]] * 3, [speed[:, cells - LANE :]] * 3)

    row_after, row_before = block_rows()
    even = is_even("section")
    sent_first[:FACE_BLOCKS] = faces_first[...]
    sent_second[:FACE_BLOCKS] = faces_second[...]

    def send(block, row, at, tail, head):
        sent_first[block, row : row + 1, at] = jnp.where(even, tail, head)
        sent_second[block, row : row + 1, at] = jnp.where(even, head, tail)

    def pack(source, turn):
        for i in range(16):
            block, row, at = strip_at(turn, i)
            send(
                block,
                row,
                at,
                source[i // 4, 3, i % 4, SUB - 1 : SUB, :],
                source[i // 4, 0, i % 4, 0:1, :],
            )

    everything = pl.ds(0, cells)
    sent_first[COEFFICIENTS] = jnp.zeros((SUB, cells), f32)
    sent_second[COEFFICIENTS] = jnp.zeros((SUB, cells), f32)
    send(COEFFICIENTS, 0, everything, visc[SUB - 1 : SUB, :], visc[0:1, :])
    send(COEFFICIENTS, 1, everything, speed[SUB - 1 : SUB, :], speed[0:1, :])
    send(COEFFICIENTS, 2, pl.ds(0, LANE), strip_v[SUB - 1 : SUB, :], strip_v[0:1, :])
    send(COEFFICIENTS, 2, pl.ds(LANE, LANE), strip_g[SUB - 1 : SUB, :], strip_g[0:1, :])

    v, g, valid = strip_v[...], strip_g[...], strip_valid()
    pack(out, 0)
    advance_strip(out, spare, v, g, valid, row_after, row_before)
    pack(spare, 1)
    advance_strip(spare, out, v, g, valid, row_after, row_before)
    pack(out, 2)
    advance_strip(out, spare, v, g, valid, row_after, row_before)
    pack(spare, 3)
    out[...] = spare[...]


def fourth_kernel(w, strip, visc, speed, strip_v, strip_g, w_out, strip_out):
    row_after, row_before = block_rows()
    advance_main(w, w_out, visc, speed, row_after, row_before)
    advance_strip(
        strip, strip_out, strip_v[...], strip_g[...], strip_valid(), row_after, row_before
    )


def edge_kernel(
    w,
    strip,
    visc,
    speed,
    strip_v,
    strip_g,
    sent_first,
    sent_second,
    got_first,
    got_second,
    out,
    e_one,
    e_two,
    z_one,
    z_two,
    e_visc,
    e_speed,
    sent,
):
    cells = w.shape[-1]
    tiles = cells // LANE
    row = iota((SUB, LANE), 0)
    lane = iota((SUB, LANE), 1)
    even = is_even("section")
    index = lax.axis_index("section")
    has_prev = index > 0
    has_next = index < lax.axis_size("section") - 1
    row_after = (row != SUB - 1) & ((row != 0) | has_prev)
    row_before = (row != 0) & ((row != SUB - 1) | has_next)

    def rows_of(own, prev_row, next_row):
        moved = jnp.where(row == 1, pltpu.roll(own, 1, 0), 0.0)
        moved = jnp.where(row == 2, pltpu.roll(own, 1, 0), moved)
        moved = jnp.where((row == 5) | (row == 6), pltpu.roll(own, SUB - 1, 0), moved)
        moved = jnp.where(row == 0, jnp.broadcast_to(prev_row, (SUB, LANE)), moved)
        return jnp.where(row == SUB - 1, jnp.broadcast_to(next_row, (SUB, LANE)), moved)

    def received(block, r, at):
        one = got_first[block, r : r + 1, at]
        two = got_second[block, r : r + 1, at]
        return jnp.where(even, two, one), jnp.where(even, one, two)

    for j in range(tiles):
        at = pl.ds(j * LANE, LANE)
        e_visc[:, at] = rows_of(visc[:, at], *received(COEFFICIENTS, 0, at))
        e_speed[:, at] = rows_of(speed[:, at], *received(COEFFICIENTS, 1, at))
    z_v = rows_of(strip_v[...], *received(COEFFICIENTS, 2, pl.ds(0, LANE)))
    z_g = rows_of(strip_g[...], *received(COEFFICIENTS, 2, pl.ds(LANE, LANE)))
    valid = strip_valid()

    def forcing(pick):
        one = jnp.broadcast_to(pick(got_first), (SUB, LANE))
        two = jnp.broadcast_to(pick(got_second), (SUB, LANE))
        own_one = jnp.broadcast_to(pick(sent_first), (SUB, LANE))
        own_two = jnp.broadcast_to(pick(sent_second), (SUB, LANE))
        from_next = jnp.where(even, one, two)
        from_prev = jnp.where(even, two, one)
        own_next = jnp.where(even, own_one, own_two)
        own_prev = jnp.where(even, own_two, own_one)
        after = jnp.where(
            row == 6, from_next, jnp.where((row == 0) & has_prev, own_prev, 0.0)
        )
        before = jnp.where(
            row == 1, from_prev, jnp.where((row == SUB - 1) & has_next, own_next, 0.0)
        )
        return after, before

    def drive(turn, comp, at, i):
        return forcing(lambda faces: face_row(faces, turn, comp, i, at))

    def drive_strip(turn, i):
        block, r, at = strip_at(turn, i)
        return forcing(lambda faces: faces[block, r : r + 1, at])

    def first_component(comp, carry):
        for j in range(tiles):
            at = pl.ds(j * LANE, LANE)
            for i in range(16):
                a, c = i // 4, i % 4
                after, before = drive(0, comp, at, i)
                e_one[comp, a, 3, c, :, at] = penalty_weight * after
                e_one[comp, a, 0, c, :, at] = penalty_weight * before
                for b in (1, 2):
                    e_one[comp, a, b, c, :, at] = jnp.zeros((SUB, LANE), f32)
        return carry

    lax.fori_loop(0, 3, first_component, 0)
    for i in range(16):
        a, c = i // 4, i % 4
        after, before = drive_strip(0, i)
        z_one[a, 3, c] = penalty_weight * after * valid
        z_one[a, 0, c] = penalty_weight * before * valid
        for b in (1, 2):
            z_one[a, b, c] = jnp.zeros((SUB, LANE), f32)

    for turn, (source, target, z_source, z_target) in enumerate(
        ((e_one, e_two, z_one, z_two), (e_two, e_one, z_two, z_one), (e_one, e_two, z_one, z_two)),
        1,
    ):
        advance_main(
            source,
            target,
            e_visc,
            e_speed,
            row_after,
            row_before,
            functools.partial(drive, turn),
        )
        advance_strip(
            z_source,
            z_target,
            z_v,
            z_g,
            valid,
            row_after,
            row_before,
            functools.partial(drive_strip, turn),
        )

    low = row < 2
    high = row >= 6

    def back(effect):
        return jnp.where(
            low, pltpu.roll(effect, SUB - 1, 0), jnp.where(high, pltpu.roll(effect, 1, 0), 0.0)
        )

    for n in range(NODES):
        a, b, c = n // 16, n // 4 % 4, n % 4
        z_one[a, b, c] = strip[a, b, c] + back(z_two[a, b, c])

    def finish(comp, carry):
        for n in range(NODES):
            a, b, c = n // 16, n // 4 % 4, n % 4
            edge = z_one[a, b, c]
            for j in range(tiles):
                at = pl.ds(j * LANE, LANE)
                value = w[comp, a, b, c, :, at] + back(e_two[comp, a, b, c, :, at])
                if j == 0:
                    value = jnp.where(lane < 4, pltpu.roll(edge, LANE - 4 - 16 * comp, 1), value)
                if j == tiles - 1:
                    value = jnp.where(
                        lane >= LANE - 4, pltpu.roll(edge, LANE - 4 - 68 - 16 * comp, 1), value
                    )
                e_one[comp, a, b, c, :, at] = value
        pltpu.make_async_copy(e_one.at[comp], out.at[comp], sent.at[comp]).start()
        return carry

    lax.fori_loop(0, 3, finish, 0)
    for comp in range(3):
        pltpu.make_async_copy(e_one.at[comp], out.at[comp], sent.at[comp]).wait()


def particle_kernel(
    fluid_hbm,
    mass_hbm,
    positions,
    velocities,
    relax_hbm,
    element_hbm,
    fill_hbm,
    visc_hbm,
    speed_hbm,
    q_out,
    parts_out,
    air_first,
    air_second,
    rates,
    strides,
    occupied,
    nodal,
    sums_even,
    sums_odd,
    totals,
    one_hot,
    rows_ref,
    fluid,
    mass,
    relax,
    element_row,
    fill_row,
    visc,
    speed,
    arrived,
):
    copies = [
        pltpu.make_async_copy(source, target, arrived.at[i])
        for i, (source, target) in enumerate(
            (
                (element_hbm, element_row),
                (fill_hbm, fill_row),
                (fluid_hbm, fluid),
                (relax_hbm, relax),
                (positions, parts_out.at[0:3]),
                (velocities, parts_out.at[3:6]),
                (mass_hbm, mass),
                (visc_hbm, visc),
                (speed_hbm, speed),
            )
        )
    ]
    for copy in copies:
        copy.start()
    sums = (sums_even, sums_odd)
    for buffer in sums:
        buffer[...] = jnp.zeros(buffer.shape, f32)
    totals[...] = jnp.zeros(totals.shape, f32)
    one_hot[...] = jnp.zeros(one_hot.shape, bf16)
    rows_ref[...] = jnp.full(rows_ref.shape, -1.0, f32)
    bins = positions.shape[1]
    groups = bins // SUB
    lanes_bins = one_hot.shape[0]
    cells = fluid.shape[-1]
    row8 = iota((SUB, LANE), 0)
    lane8 = iota((SUB, LANE), 1)
    same = (lane8 % SUB == row8).astype(f32)

    copies[0].wait()
    copies[1].wait()

    rows_ref[0:1, :bins] = element_row[...].astype(f32)
    rows_ref[1:2, :bins] = fill_row[...].astype(f32)
    element_lanes = rows_ref[0:1, :]
    section_lanes = jnp.zeros_like(element_lanes)
    for s in range(1, SUB):
        section_lanes = section_lanes + (element_lanes >= float(s * cells)).astype(f32)

    lane_bins = iota((SUB, lanes_bins), 1)
    row_bins = iota((SUB, lanes_bins), 0)
    for g in range(groups):
        own = lane_bins == row_bins + g * SUB
        element = jnp.sum(jnp.where(own, element_lanes, 0.0), axis=1, keepdims=True)
        fill = jnp.sum(jnp.where(own, rows_ref[1:2, :], 0.0), axis=1, keepdims=True)
        section = jnp.zeros_like(element)
        for s in range(1, SUB):
            section = section + (element >= float(s * cells)).astype(f32)
        column = element - section * float(cells)
        at = pl.ds(g * SUB, SUB)
        occ = (lane8.astype(f32) < fill).astype(f32)
        occupied[at, :] = occ
        strides[at, :] = occ * stride_step
        hot = (iota((SUB, cells), 1).astype(f32) == column).astype(f32)
        one_hot[at, :] = hot.astype(bf16)

    copies[2].wait()

    spread = (iota((LANE, LANE), 0) // SUB == iota((LANE, LANE), 1) // SUB).astype(bf16)
    in_section_rows = (iota((LANE, lanes_bins), 0) % SUB).astype(f32) == section_lanes
    hot_all = one_hot[...]
    sources = []
    for comp in range(3):
        for a in range(4):
            sources += split(fluid[comp, a].reshape(16 * SUB, cells))
    found = dot_t(jnp.concatenate(sources, axis=0), hot_all)
    picked = [
        jnp.where(in_section_rows, found[k * LANE : (k + 1) * LANE], 0.0).T.astype(bf16)
        for k in range(24)
    ]
    wide = dot(jnp.concatenate(picked, axis=0), spread)
    for i in range(12):
        for part in range(2):
            rows = wide[(i * 2 + part) * lanes_bins : (i * 2 + part + 1) * lanes_bins]
            for g in range(groups):
                block = rows[g * SUB : (g + 1) * SUB, :] * same
                start = part * 96 + i * SUB
                nodal[g, start : start + SUB, :] = block.astype(bf16)

    for copy in copies[3:]:
        copy.wait()
    rates[...] = relax[...] * occupied[...]

    def sum_lanes(first, turn):
        buffer = sums[first // GROUPS_TOGETHER % 2]
        for slot in range(GROUPS_TOGETHER):
            at = pl.ds((first + slot) * SUB, SUB)
            total = totals[turn // 8, at, :]
            for n in range(16):
                j = turn * 16 + n
                over_lanes = jnp.sum(buffer[slot, j], axis=1, keepdims=True)
                total = jnp.where(lane8 == j % LANE, over_lanes, total)
                buffer[slot, j] = jnp.zeros((SUB, LANE), f32)
            totals[turn // 8, at, :] = total

    def substep(first, turn, carry):
        if first:
            sum_lanes(first - GROUPS_TOGETHER, turn)
        buffer = sums[first // GROUPS_TOGETHER % 2]
        for slot in range(GROUPS_TOGETHER):
            g = first + slot
            at = pl.ds(g * SUB, SUB)
            x = [parts_out[k, at, :] for k in range(3)]
            v = [parts_out[3 + k, at, :] for k in range(3)]
            rate = rates[at, :]
            step = strides[at, :]
            occ = occupied[at, :]
            la, lb, lc = [basis_values(x[k]) for k in range(3)]
            across = [lb[b] * lc[c] for b in range(4) for c in range(4)]
            high, low = split(jnp.concatenate(across, axis=0))
            by_high = dot(nodal[g], high)
            at_a = by_high[:96] + (by_high[96:] + dot(nodal[g, :96], low))
            pushes = []
            for k in range(3):
                rows = [at_a[(k * 4 + a) * SUB : (k * 4 + a + 1) * SUB, :] for a in range(4)]
                u = (la[0] * rows[0] + la[1] * rows[1]) + (la[2] * rows[2] + la[3] * rows[3])
                dv = rate * (u - v[k])
                moved = v[k] + dv
                parts_out[3 + k, at, :] = moved
                parts_out[k, at, :] = jnp.clip(x[k] + step * moved, -1.0, 1.0)
                pushes += [la[a] * dv for a in range(4)]
            weighs = [la[a] * la[a] * occ for a in range(4)]
            for n in range(16):
                for i in range(12):
                    j = i * 16 + n
                    buffer[slot, j] = buffer[slot, j] + across[n] * pushes[i]
            for n in range(16):
                square = across[n] * across[n]
                for a in range(4):
                    j = (12 + a) * 16 + n
                    buffer[slot, j] = buffer[slot, j] + square * weighs[a]
        return carry

    for first in range(0, groups, GROUPS_TOGETHER):
        lax.fori_loop(0, SUBSTEPS, functools.partial(substep, first), 0)
    for turn in range(16):
        sum_lanes(groups - GROUPS_TOGETHER, turn)

    spread_rows = (iota((LANE, 16), 0) // SUB == iota((LANE, 16), 1)).astype(bf16)
    by_node = jnp.concatenate([totals[0].T, totals[1].T], axis=0)

    for a in range(4):
        highs = []
        lows = []
        for i in (12 + a, a, 4 + a, 8 + a):
            high, low = split(by_node[i * 16 : (i + 1) * 16, :])
            wide = dot(spread_rows, high) + dot(spread_rows, low)
            high, low = split(jnp.where(in_section_rows, wide, 0.0))
            highs.append(high)
            lows.append(low)
        placed = dot(jnp.concatenate(highs + lows, axis=0), hot_all)
        placed = (placed[: 4 * LANE] + placed[4 * LANE :]).reshape(4, 4, 4, SUB, cells)
        scale = 1.0 / (mass[...][None, None] + placed[0])
        for comp in range(3):
            q_out[comp, a] = fluid[comp, a] - placed[1 + comp] * scale

    pack_columns(q_out, visc, speed, air_first, air_second)


def swap(values, axis, offset):
    count = lax.axis_size(axis)
    pairs = []
    for i in range(offset, count - 1, 2):
        pairs += [(i, i + 1), (i + 1, i)]
    return lax.ppermute(values, axis, pairs)


def local(
    fluid_velocity,
    viscosity,
    axial_speed,
    fluid_mass,
    positions,
    velocities,
    relax_rates,
    bin_element,
    bin_fill,
):
    sec_cells, air_cells = fluid_velocity.shape[2:]
    bins = positions.shape[0]
    groups = bins // SUB
    lanes_bins = -(-bins // LANE) * LANE
    field_shape = (3, 4, 4, 4, sec_cells, air_cells)
    field = jax.ShapeDtypeStruct(field_shape, f32)
    air_shape = jax.ShapeDtypeStruct((9, SUB, LANE), f32)
    strip_shape = jax.ShapeDtypeStruct((4, 4, 4, SUB, LANE), f32)
    tile_shape = jax.ShapeDtypeStruct((SUB, LANE), f32)
    face_shape = jax.ShapeDtypeStruct((FACE_BLOCKS, SUB, air_cells), f32)
    sent_shape = jax.ShapeDtypeStruct((COEFFICIENTS + 1, SUB, air_cells), f32)
    vmem = pl.BlockSpec(memory_space=pltpu.VMEM)
    hbm = pl.BlockSpec(memory_space=pltpu.HBM)
    params = pltpu.CompilerParams(vmem_limit_bytes=48 * 1024 * 1024)
    q, particles_out, air_first, air_second = pl.pallas_call(
        particle_kernel,
        out_shape=(field, jax.ShapeDtypeStruct((6, bins, LANE), f32), air_shape, air_shape),
        in_specs=[hbm] * 9,
        out_specs=(vmem,) * 4,
        scratch_shapes=[
            pltpu.VMEM((bins, LANE), f32),
            pltpu.VMEM((bins, LANE), f32),
            pltpu.VMEM((bins, LANE), f32),
            pltpu.VMEM((groups, 192, LANE), bf16),
            pltpu.VMEM((GROUPS_TOGETHER, 256, SUB, LANE), f32),
            pltpu.VMEM((GROUPS_TOGETHER, 256, SUB, LANE), f32),
            pltpu.VMEM((2, lanes_bins, LANE), f32),
            pltpu.VMEM((lanes_bins, air_cells), bf16),
            pltpu.VMEM((SUB, lanes_bins), f32),
            pltpu.VMEM(field_shape, f32),
            pltpu.VMEM(fluid_mass.shape, f32),
            pltpu.VMEM(relax_rates.shape, f32),
            pltpu.VMEM((1, bins), jnp.int32),
            pltpu.VMEM((1, bins), jnp.int32),
            pltpu.VMEM(viscosity.shape, f32),
            pltpu.VMEM(axial_speed.shape, f32),
            pltpu.SemaphoreType.DMA((9,)),
        ],
        compiler_params=params,
        name="particles",
    )(
        *(
            pltpu.with_memory_space_constraint(array, pltpu.HBM)
            for array in (
                fluid_velocity.reshape(field_shape),
                fluid_mass,
                positions.transpose(1, 0, 2),
                velocities.transpose(1, 0, 2),
                relax_rates,
                bin_element.reshape(1, bins),
                bin_fill.reshape(1, bins),
                viscosity,
                axial_speed,
            )
        )
    )

    def call(kernel, name, outputs, scratch, *operands, place=None, more=()):
        return pl.pallas_call(
            kernel,
            out_shape=outputs,
            in_specs=[vmem] * len(operands),
            out_specs=jax.tree.map(lambda _: place or vmem, outputs),
            scratch_shapes=[pltpu.VMEM(shape.shape, f32) for shape in scratch] + list(more),
            compiler_params=params,
            cost_estimate=pl.CostEstimate(
                flops=30 * fluid_velocity.size, bytes_accessed=8 * fluid_velocity.size, transcendentals=0
            ),
            name=name,
        )(*operands)

    got_air = (swap(air_first, "airway", 0), swap(air_second, "airway", 1))
    w, *faces = call(
        main_kernel, "main", (field, face_shape, face_shape), (field,), q, viscosity, axial_speed
    )
    strip, strip_v, strip_g, *sent = call(
        strip_kernel,
        "strip",
        (strip_shape, tile_shape, tile_shape, sent_shape, sent_shape),
        (strip_shape,),
        q,
        viscosity,
        axial_speed,
        *got_air,
        *faces,
    )
    got = (swap(sent[0], "section", 0), swap(sent[1], "section", 1))
    w, strip = call(
        fourth_kernel,
        "fourth",
        (field, strip_shape),
        (),
        w,
        strip,
        viscosity,
        axial_speed,
        strip_v,
        strip_g,
    )
    mass_tile = jax.ShapeDtypeStruct(fluid_mass.shape, f32)
    q = call(
        edge_kernel,
        "edge",
        field,
        (field, field, strip_shape, strip_shape, mass_tile, mass_tile),
        w,
        strip,
        viscosity,
        axial_speed,
        strip_v,
        strip_g,
        *sent,
        *got,
        place=hbm,
        more=(pltpu.SemaphoreType.DMA((3,)),),
    )
    return (q.reshape(3, NODES, sec_cells, air_cells), particles_out.transpose(1, 0, 2))


def solution(mesh):
    return jax.shard_map(
        local,
        mesh=mesh,
        in_specs=(
            P(None, None, "section", "airway"),
            P("section", "airway"),
            P("section", "airway"),
            P("section", "airway"),
            P(("airway", "section"), None, None),
            P(("airway", "section"), None, None),
            P(("airway", "section"), None),
            P(("airway", "section")),
            P(("airway", "section")),
        ),
        out_specs=(P(None, None, "section", "airway"), P(("airway", "section"), None, None)),
        check_vma=False,
    )
```
